32 devices in a mesh: seq: 8 (over z, y), dp: 4 (over x, core).
Axes of the slice: x: 2, y: 2, z: 4, core: 2. Of those that a mesh axis runs over, the one named last changes fastest.
Arguments:
- gate_in: bfloat16 [4, 2048, 1024], P('dp', None, 'seq'), may hold values from -6 to 6
- values_in: bfloat16 [4, 2048, 1024], P('dp', None, 'seq'), may hold values from -6 to 6
- out_grad: bfloat16 [4, 2048, 1024], P('dp', None, 'seq'), may hold values from -0.1875 to 0.1875
- filter_taps: float32 [2048, 1024], P(None, 'seq'), may hold values from -6 to 6
Outputs:
- grad_gate: bfloat16 [4, 2048, 1024], P('dp', None, 'seq')
- grad_values: bfloat16 [4, 2048, 1024], P('dp', None, 'seq')
- grad_filter: float32 [2048, 1024], P('dp', 'seq')
The draws below stay inside these ranges and needn't reach their ends.
All inputs are finite; a program needn't handle non-finite values.
Results may differ from the reference program's by a relative error of at most 0.005.
Values may be sent and summed in bfloat16 or wider, within the bound.
No kernel may reach another device: no remote copies, remote signals or barrier semaphores. Data moves between devices by JAX's collectives and lax.ppermute only.
A program may use at most 128 MiB of HBM per device.

```python
import jax
import jax.numpy as jnp
from jax import lax

C = 2048
LENGTH = 1024
SEQS = 4


def shard_levels(key, dims, split, low, high):
    level, own = 1.0, jax.random.fold_in(key, 6)
    for position, blocks in split:
        draws = jnp.exp(jax.random.uniform(jax.random.fold_in(own, position), (blocks,), jnp.float32, low / len(split), high / len(split)))
        level = level * jnp.repeat(draws, dims[position] // blocks).reshape([-1 if axis == position else 1 for axis in range(len(dims))])
    return level


def normal_values(key, shape, deviation, most, shards=(), kind=jnp.bfloat16):
    entries = deviation * jax.random.normal(key, shape, jnp.float32)
    if shards:
        entries = entries * shard_levels(key, shape, shards, -0.22, 0.18)
    return jnp.clip(entries, -most, most).astype(kind)


def setup_inputs(seed: int = 0) -> dict:
    key_of = jax.random.split(jax.random.key(seed), 5)
    return {
        "gate_in": normal_values(key_of[0], (SEQS, C, LENGTH), 1.0, 6.0, ((0, 4), (2, 8))),
        "values_in": normal_values(key_of[1], (SEQS, C, LENGTH), 1.0, 6.0, ((0, 4), (2, 8))),
        "out_grad": normal_values(key_of[2], (SEQS, C, LENGTH), LENGTH ** -0.5, 0.1875, ((0, 4), (2, 8))),
        "filter_taps": normal_values(key_of[3], (C, LENGTH), 1.0, 6.0, ((1, 8),), jnp.float32),
    }


def reference(gate_in, values_in, out_grad, filter_taps):
    mixed = (gate_in.astype(jnp.float32) * values_in.astype(jnp.float32)).astype(jnp.bfloat16)
    seq_total = out_grad.shape[0]
    channels = out_grad.shape[1]
    length = out_grad.shape[2]
    doubled = 2 * length
    block = 128
    blocks = channels // block

    def per_block(start):
        grads = lax.dynamic_slice_in_dim(out_grad, start, block, 1).astype(jnp.float32)
        inputs = lax.dynamic_slice_in_dim(mixed, start, block, 1).astype(jnp.float32)
        filter_rows = lax.dynamic_slice_in_dim(filter_taps, start, block, 0)
        grad_spec = jnp.fft.fft(grads, n=doubled, axis=2)
        input_spec = jnp.fft.fft(inputs, n=doubled, axis=2)
        filter_spec = jnp.fft.fft(filter_rows, n=doubled, axis=1)
        carried = jnp.fft.ifft(jnp.conj(filter_spec)[None] * grad_spec, axis=2).real[:, :, :length]
        lagged = jnp.fft.ifft(jnp.sum(grad_spec * jnp.conj(input_spec), axis=0), axis=1).real[:, :length]
        return carried.astype(jnp.float32), lagged.astype(jnp.float32)

    starts = jnp.arange(blocks, dtype=jnp.int32) * block
    carried, lagged = lax.map(per_block, starts)
    carried = jnp.transpose(carried, (1, 0, 2, 3)).reshape(seq_total, channels, length).astype(jnp.bfloat16)
    grad_filter = lagged.reshape(channels, length)
    carried_wide = carried.astype(jnp.float32)
    grad_gate = (carried_wide * values_in.astype(jnp.float32)).astype(jnp.bfloat16)
    grad_values = (carried_wide * gate_in.astype(jnp.float32)).astype(jnp.bfloat16)
    return grad_gate, grad_values, grad_filter
```

```python
import functools
import math

import jax
import jax.numpy as jnp
from jax import lax
from jax.experimental import pallas as pl
from jax.experimental.pallas import tpu as pltpu
from jax.sharding import PartitionSpec as P

LANES = 128
SUBLANES = 16
ROOM = 40 * 2**20

precise = lax.Precision.HIGHEST
coarse = lax.Precision.HIGH


def spin_tables(count_in, count_out, period):
    rows = lax.broadcasted_iota(jnp.int32, (count_in, count_out), 0)
    cols = lax.broadcasted_iota(jnp.int32, (count_in, count_out), 1)
    phase = (rows * cols % period).astype(jnp.float32) * (2.0 * math.pi / period)
    return (jnp.cos(phase), jnp.sin(phase))


def make_tables(length, columns):
    rows_in = length // columns
    rows_out = 2 * rows_in
    first_cos, first_sin = spin_tables(rows_in, rows_out, rows_out)
    turn = spin_tables(rows_out, columns, 2 * length)
    last_cos, last_sin = spin_tables(columns, columns, columns)
    first_fwd = jnp.concatenate([first_cos, -first_sin], axis=1)
    last_fwd = jnp.concatenate(
        [
            jnp.concatenate([last_cos, -last_sin], axis=1),
            jnp.concatenate([last_sin, last_cos], axis=1),
        ],
        axis=0,
    )
    last_inv = jnp.concatenate(
        [
            jnp.concatenate([last_cos.T, last_sin.T], axis=1),
            jnp.concatenate([-last_sin.T, last_cos.T], axis=1),
        ],
        axis=0,
    )
    first_inv = jnp.concatenate(
        [
            jnp.concatenate([first_cos.T, first_sin.T], axis=1),
            jnp.concatenate([-first_sin.T, first_cos.T], axis=1),
        ],
        axis=0,
    )
    return (first_fwd, turn, last_fwd, last_inv, first_inv)


def spectrum(signal, tables, columns, first_precision):
    first_fwd, (turn_cos, turn_sin), last_fwd, last_inv, first_inv = tables
    held, length = signal.shape
    half = turn_cos.shape[0]
    grid = signal.reshape(held, length // columns, columns)
    part = jnp.einsum("cmn,mk->ckn", grid, first_fwd, precision=first_precision)
    part_real = part[:, :half]
    part_imag = part[:, half:]
    turned = jnp.concatenate(
        [part_real * turn_cos + part_imag * turn_sin, part_imag * turn_cos - part_real * turn_sin],
        axis=2,
    )
    out = jnp.einsum("ckn,nj->ckj", turned, last_fwd, precision=first_precision)
    return (out[:, :, :columns], out[:, :, columns:])


def to_signal(spec_real, spec_imag, tables, length):
    first_fwd, (turn_cos, turn_sin), last_fwd, last_inv, first_inv = tables
    held = spec_real.shape[0]
    columns = spec_real.shape[2]
    rows_in = length // columns
    stacked = jnp.concatenate([spec_real, spec_imag], axis=2)
    back = jnp.einsum("ckj,jn->ckn", stacked, last_inv, precision=coarse)
    back_real = back[:, :, :columns]
    back_imag = back[:, :, columns:]
    turned = jnp.concatenate(
        [back_real * turn_cos - back_imag * turn_sin, back_imag * turn_cos + back_real * turn_sin],
        axis=1,
    )
    factor = 1.0 / (2 * length)
    both = jnp.einsum("ckn,km->cmn", turned, first_inv, precision=coarse) * factor
    real_part = both[:, :rows_in]
    imag_part = both[:, rows_in:]
    return (real_part.reshape(held, length), imag_part.reshape(held, length))


def spectral_shards(gate_in, values_in, out_grad, filter_taps):
    seq_count = lax.axis_size("seq")
    group_count = lax.axis_size("dp")
    channels = gate_in.shape[1]
    shard_len = gate_in.shape[2]
    length = shard_len * seq_count
    quarter = channels // group_count
    per_block = quarter // seq_count
    held_channels = group_count * per_block
    columns = 128 if length % 128 == 0 and length >= 8192 else 32
    tables = make_tables(length, columns)
    gate_wide = gate_in[0].astype(jnp.float32)
    values_wide = values_in[0].astype(jnp.float32)
    mixed = (gate_wide * values_wide).astype(jnp.bfloat16)
    grad_rows, mixed_rows = (
        lax.all_to_all(
            out_grad[0].reshape(group_count, quarter, shard_len),
            "seq",
            split_axis=1,
            concat_axis=2,
            tiled=True,
        ),
        lax.all_to_all(
            mixed.reshape(group_count, quarter, shard_len),
            "seq",
            split_axis=1,
            concat_axis=2,
            tiled=True,
        ),
    )
    filter_grouped = filter_taps.reshape(group_count, quarter, shard_len)
    filter_rows = lax.all_to_all(filter_grouped, "seq", split_axis=1, concat_axis=2, tiled=True)
    grad_real, grad_imag = spectrum(
        grad_rows.reshape(held_channels, length).astype(jnp.float32), tables, columns, coarse
    )
    mix_real, mix_imag = spectrum(
        mixed_rows.reshape(held_channels, length).astype(jnp.float32), tables, columns, coarse
    )
    tap_real, tap_imag = spectrum(
        filter_rows.reshape(held_channels, length), tables, columns, precise
    )
    carry_real = tap_real * grad_real + tap_imag * grad_imag
    carry_imag = tap_real * grad_imag - tap_imag * grad_real
    lag_real = grad_real * mix_real + grad_imag * mix_imag
    lag_imag = grad_imag * mix_real - grad_real * mix_imag
    carried, lagged = to_signal(carry_real - lag_imag, carry_imag + lag_real, tables, length)
    carried = carried.astype(jnp.bfloat16).reshape(group_count, per_block, length)
    returned = lax.all_to_all(carried, "seq", split_axis=2, concat_axis=1, tiled=True)
    carried_home = returned.reshape(channels, shard_len).astype(jnp.float32)
    lagged = lagged.reshape(group_count, per_block, length)
    summed = lax.psum_scatter(lagged, "dp", scatter_dimension=0, tiled=True)
    grad_filter = lax.all_to_all(summed, "seq", split_axis=2, concat_axis=1, tiled=True).reshape(
        quarter, shard_len
    )
    grad_gate = (carried_home * values_wide).astype(jnp.bfloat16)[None]
    grad_values = (carried_home * gate_wide).astype(jnp.bfloat16)[None]
    return (grad_gate, grad_values, grad_filter)


def pack_body(groups, peers, own_ref, gate_ref, values_ref, grad_ref, taps_ref, out_ref):
    part = out_ref.shape[1] // (2 * groups + 2)
    half = groups * part
    for q in range(groups):
        rows = pl.ds(q * peers * part, peers * part)
        mixed = gate_ref[rows, :].astype(jnp.float32) * values_ref[rows, :].astype(jnp.float32)
        out_ref[:, q * part : (q + 1) * part, :] = grad_ref[rows, :].reshape(peers, part, LANES)
        out_ref[:, half + q * part : half + (q + 1) * part, :] = mixed.astype(jnp.bfloat16).reshape(
            peers, part, LANES
        )
    first = pl.multiple_of(own_ref[0] * (peers * part), peers * part)
    taps = taps_ref[pl.ds(first, peers * part), :]
    high = taps.astype(jnp.bfloat16)
    low = (taps - high.astype(jnp.float32)).astype(jnp.bfloat16)
    out_ref[:, 2 * half : 2 * half + part, :] = high.reshape(peers, part, LANES)
    out_ref[:, 2 * half + part :, :] = low.reshape(peers, part, LANES)


def correlate_body(seqs, blocks, in_ref, out_ref, gs, ms, fs, cs, rs):
    peers = seqs * blocks
    part = in_ref.shape[1] // (2 * seqs + 2)
    held = seqs * part
    row = lax.broadcasted_iota(jnp.int32, (LANES, LANES), 0)
    lane = lax.broadcasted_iota(jnp.int32, (LANES, LANES), 1)
    flip = jnp.where(row + lane == LANES - 1, 1.0, 0.0).astype(jnp.bfloat16)
    same = lane <= row
    ahead = lane >= row
    span = blocks * held
    for b in range(seqs):
        mine = slice(b * blocks, (b + 1) * blocks)
        gs[pl.ds(2 * b * span, span), :] = (
            in_ref[mine, :held, :].astype(jnp.float32).reshape(span, LANES)
        )
        gs[pl.ds((2 * b + 1) * span, span), :] = jnp.zeros((span, LANES), jnp.float32)
        ms[pl.ds(b * span, span), :] = (
            in_ref[mine, held : 2 * held, :].astype(jnp.float32).reshape(span, LANES)
        )
        for s in range(blocks):
            high = in_ref[b * blocks + s, 2 * held : 2 * held + part, :].astype(jnp.float32)
            low = in_ref[b * blocks + s, 2 * held + part :, :].astype(jnp.float32)
            fs[pl.ds(s * held + b * part, part), :] = high + low

    def channel(c, carry):
        shifted = []
        for k in range(blocks):
            parts = [
                gs[pl.ds((2 * b * blocks + k) * held + c, blocks, stride=held), :] for b in range(seqs)
            ]
            shifted.append(jnp.concatenate(parts, axis=0).astype(jnp.bfloat16))
        hankel = jnp.concatenate(shifted, axis=1)
        mixed = ms[pl.ds(c, peers, stride=held), :].astype(jnp.bfloat16)
        dims = (((1,), (1,)), ((), ()))
        turned = lax.dot_general(flip, mixed, dims, preferred_element_type=jnp.float32).astype(
            jnp.bfloat16
        )
        gram = jnp.dot(turned, hankel, preferred_element_type=jnp.float32)
        rolled = [
            pltpu.roll(gram[:, k * LANES : (k + 1) * LANES], 1, 1, stride=1, stride_axis=0)
            for k in range(blocks)
        ]
        rolled.append(jnp.zeros((LANES, LANES), jnp.float32))
        sums = [
            jnp.sum(jnp.where(same, rolled[k], rolled[k + 1]), axis=0, keepdims=True)
            for k in range(blocks)
        ]
        rs[pl.ds(c, blocks, stride=held), :] = jnp.concatenate(sums, axis=0)
        taps = fs[pl.ds(c, blocks, stride=held), :]
        before = jnp.zeros((LANES, LANES), jnp.float32)
        high, low = [], []
        for k in range(blocks):
            turn = pltpu.roll(
                jnp.broadcast_to(taps[k : k + 1, :], (LANES, LANES)), 0, 1, stride=1, stride_axis=0
            )
            block = jnp.where(ahead, turn, before)
            before = turn
            top = block.astype(jnp.bfloat16)
            high.append(top)
            low.append((block - top.astype(jnp.float32)).astype(jnp.bfloat16))
        carried = lax.dot_general(
            hankel, jnp.concatenate(high, axis=1), dims, preferred_element_type=jnp.float32
        ) + lax.dot_general(
            hankel, jnp.concatenate(low, axis=1), dims, preferred_element_type=jnp.float32
        )
        cs[pl.ds(c, peers, stride=held), :] = carried
        return carry

    lax.fori_loop(0, held, channel, 0)
    out_ref[:, :held, :] = cs[...].reshape(peers, held, LANES).astype(jnp.bfloat16)
    for q in range(seqs):
        for s in range(blocks):
            out_ref[q * blocks + s, held:, :] = rs[pl.ds(s * held + q * part, part), :].astype(
                jnp.bfloat16
            )


def unpack_body(groups, in_ref, gate_ref, values_ref, gate_out, values_out, filter_out):
    peers = in_ref.shape[0]
    part = in_ref.shape[1] // (groups + 1)
    for q in range(groups):
        rows = pl.ds(q * peers * part, peers * part)
        carried = (
            in_ref[:, q * part : (q + 1) * part, :].astype(jnp.float32).reshape(peers * part, LANES)
        )
        gate_out[rows, :] = (carried * values_ref[rows, :].astype(jnp.float32)).astype(jnp.bfloat16)
        values_out[rows, :] = (carried * gate_ref[rows, :].astype(jnp.float32)).astype(jnp.bfloat16)
    filter_out[...] = (
        in_ref[:, groups * part :, :].astype(jnp.float32).reshape(peers * part, LANES)
    )


def correlate(arrived, seqs):
    peers, rows, _ = arrived.shape
    blocks = peers // seqs
    part = rows // (2 * seqs + 2)
    held = seqs * part
    whole = pl.BlockSpec(memory_space=pltpu.VMEM)
    return pl.pallas_call(
        functools.partial(correlate_body, seqs, blocks),
        out_shape=jax.ShapeDtypeStruct((peers, held + part, LANES), jnp.bfloat16),
        in_specs=[whole],
        out_specs=whole,
        scratch_shapes=[
            pltpu.VMEM((2 * peers * held, LANES), jnp.float32),
            pltpu.VMEM((peers * held, LANES), jnp.float32),
            pltpu.VMEM((blocks * held, LANES), jnp.float32),
            pltpu.VMEM((peers * held, LANES), jnp.float32),
            pltpu.VMEM((blocks * held, LANES), jnp.float32),
        ],
        cost_estimate=pl.CostEstimate(
            flops=6 * held * LANES * blocks * LANES * peers, bytes_accessed=4 * arrived.size, transcendentals=0
        ),
    )(arrived)


def direct_shards(gate_in, values_in, out_grad, filter_taps):
    groups = lax.axis_size("dp")
    peers = groups * lax.axis_size("seq")
    channels = gate_in.shape[1]
    part = channels // (groups * peers)
    whole = pl.BlockSpec(memory_space=pltpu.VMEM)
    own = lax.axis_index("dp").astype(jnp.int32).reshape(1)
    packed = pl.pallas_call(
        functools.partial(pack_body, groups, peers),
        out_shape=jax.ShapeDtypeStruct((peers, (2 * groups + 2) * part, LANES), jnp.bfloat16),
        in_specs=[pl.BlockSpec(memory_space=pltpu.SMEM), whole, whole, whole, whole],
        out_specs=whole,
    )(own, gate_in[0], values_in[0], out_grad[0], filter_taps)
    arrived = lax.all_to_all(packed, ("dp", "seq"), split_axis=0, concat_axis=0, tiled=True)
    made = correlate(arrived, groups)
    home = lax.all_to_all(made, ("dp", "seq"), split_axis=0, concat_axis=0, tiled=True)
    wide = jax.ShapeDtypeStruct((channels, LANES), jnp.bfloat16)
    grad_gate, grad_values, grad_filter = pl.pallas_call(
        functools.partial(unpack_body, groups),
        out_shape=(wide, wide, jax.ShapeDtypeStruct((channels // groups, LANES), jnp.float32)),
        in_specs=[whole, whole, whole],
        out_specs=(whole, whole, whole),
    )(home, gate_in[0], values_in[0])
    return (grad_gate[None], grad_values[None], grad_filter)


def shards(gate_in, values_in, out_grad, filter_taps):
    groups = lax.axis_size("dp")
    peers = groups * lax.axis_size("seq")
    channels, shard_len = gate_in.shape[1:]
    part = channels // (groups * peers)
    fits = 24 * channels * LANES * groups <= ROOM
    if shard_len == LANES and channels == part * groups * peers and part % SUBLANES == 0 and fits:
        return direct_shards(gate_in, values_in, out_grad, filter_taps)
    return spectral_shards(gate_in, values_in, out_grad, filter_taps)


def solution(mesh):
    return jax.shard_map(
        shards,
        mesh=mesh,
        in_specs=(P("dp", None, "seq"), P("dp", None, "seq"), P("dp", None, "seq"), P(None, "seq")),
        out_specs=(P("dp", None, "seq"), P("dp", None, "seq"), P("dp", "seq")),
        check_vma=False,
    )
```

```python
import functools
import math

import jax
import jax.numpy as jnp
from jax import lax
from jax.experimental import pallas as pl
from jax.experimental.pallas import tpu as pltpu
from jax.sharding import PartitionSpec as P

LANES = 128
SUBLANES = 16
REACH = 32
UNROLL = 8
ROOM = 40 * 2**20

precise = lax.Precision.HIGHEST
coarse = lax.Precision.HIGH


def spin_tables(count_in, count_out, period):
    rows = lax.broadcasted_iota(jnp.int32, (count_in, count_out), 0)
    cols = lax.broadcasted_iota(jnp.int32, (count_in, count_out), 1)
    phase = (rows * cols % period).astype(jnp.float32) * (2.0 * math.pi / period)
    return (jnp.cos(phase), jnp.sin(phase))


def make_tables(length, columns):
    rows_in = length // columns
    rows_out = 2 * rows_in
    first_cos, first_sin = spin_tables(rows_in, rows_out, rows_out)
    turn = spin_tables(rows_out, columns, 2 * length)
    last_cos, last_sin = spin_tables(columns, columns, columns)
    first_fwd = jnp.concatenate([first_cos, -first_sin], axis=1)
    last_fwd = jnp.concatenate(
        [
            jnp.concatenate([last_cos, -last_sin], axis=1),
            jnp.concatenate([last_sin, last_cos], axis=1),
        ],
        axis=0,
    )
    last_inv = jnp.concatenate(
        [
            jnp.concatenate([last_cos.T, last_sin.T], axis=1),
            jnp.concatenate([-last_sin.T, last_cos.T], axis=1),
        ],
        axis=0,
    )
    first_inv = jnp.concatenate(
        [
            jnp.concatenate([first_cos.T, first_sin.T], axis=1),
            jnp.concatenate([-first_sin.T, first_cos.T], axis=1),
        ],
        axis=0,
    )
    return (first_fwd, turn, last_fwd, last_inv, first_inv)


def spectrum(signal, tables, columns, first_precision):
    first_fwd, (turn_cos, turn_sin), last_fwd, last_inv, first_inv = tables
    held, length = signal.shape
    half = turn_cos.shape[0]
    grid = signal.reshape(held, length // columns, columns)
    part = jnp.einsum("cmn,mk->ckn", grid, first_fwd, precision=first_precision)
    part_real = part[:, :half]
    part_imag = part[:, half:]
    turned = jnp.concatenate(
        [part_real * turn_cos + part_imag * turn_sin, part_imag * turn_cos - part_real * turn_sin],
        axis=2,
    )
    out = jnp.einsum("ckn,nj->ckj", turned, last_fwd, precision=first_precision)
    return (out[:, :, :columns], out[:, :, columns:])


def to_signal(spec_real, spec_imag, tables, length):
    first_fwd, (turn_cos, turn_sin), last_fwd, last_inv, first_inv = tables
    held = spec_real.shape[0]
    columns = spec_real.shape[2]
    rows_in = length // columns
    stacked = jnp.concatenate([spec_real, spec_imag], axis=2)
    back = jnp.einsum("ckj,jn->ckn", stacked, last_inv, precision=coarse)
    back_real = back[:, :, :columns]
    back_imag = back[:, :, columns:]
    turned = jnp.concatenate(
        [back_real * turn_cos - back_imag * turn_sin, back_imag * turn_cos + back_real * turn_sin],
        axis=1,
    )
    factor = 1.0 / (2 * length)
    both = jnp.einsum("ckn,km->cmn", turned, first_inv, precision=coarse) * factor
    real_part = both[:, :rows_in]
    imag_part = both[:, rows_in:]
    return (real_part.reshape(held, length), imag_part.reshape(held, length))


def spectral_shards(gate_in, values_in, out_grad, filter_taps):
    seq_count = lax.axis_size("seq")
    group_count = lax.axis_size("dp")
    channels = gate_in.shape[1]
    shard_len = gate_in.shape[2]
    length = shard_len * seq_count
    quarter = channels // group_count
    per_block = quarter // seq_count
    held_channels = group_count * per_block
    columns = 128 if length % 128 == 0 and length >= 8192 else 32
    tables = make_tables(length, columns)
    gate_wide = gate_in[0].astype(jnp.float32)
    values_wide = values_in[0].astype(jnp.float32)
    mixed = (gate_wide * values_wide).astype(jnp.bfloat16)
    grad_rows, mixed_rows = (
        lax.all_to_all(
            out_grad[0].reshape(group_count, quarter, shard_len),
            "seq",
            split_axis=1,
            concat_axis=2,
            tiled=True,
        ),
        lax.all_to_all(
            mixed.reshape(group_count, quarter, shard_len),
            "seq",
            split_axis=1,
            concat_axis=2,
            tiled=True,
        ),
    )
    filter_grouped = filter_taps.reshape(group_count, quarter, shard_len)
    filter_rows = lax.all_to_all(filter_grouped, "seq", split_axis=1, concat_axis=2, tiled=True)
    grad_real, grad_imag = spectrum(
        grad_rows.reshape(held_channels, length).astype(jnp.float32), tables, columns, coarse
    )
    mix_real, mix_imag = spectrum(
        mixed_rows.reshape(held_channels, length).astype(jnp.float32), tables, columns, coarse
    )
    tap_real, tap_imag = spectrum(
        filter_rows.reshape(held_channels, length), tables, columns, precise
    )
    carry_real = tap_real * grad_real + tap_imag * grad_imag
    carry_imag = tap_real * grad_imag - tap_imag * grad_real
    lag_real = grad_real * mix_real + grad_imag * mix_imag
    lag_imag = grad_imag * mix_real - grad_real * mix_imag
    carried, lagged = to_signal(carry_real - lag_imag, carry_imag + lag_real, tables, length)
    carried = carried.astype(jnp.bfloat16).reshape(group_count, per_block, length)
    returned = lax.all_to_all(carried, "seq", split_axis=2, concat_axis=1, tiled=True)
    carried_home = returned.reshape(channels, shard_len).astype(jnp.float32)
    lagged = lagged.reshape(group_count, per_block, length)
    summed = lax.psum_scatter(lagged, "dp", scatter_dimension=0, tiled=True)
    grad_filter = lax.all_to_all(summed, "seq", split_axis=2, concat_axis=1, tiled=True).reshape(
        quarter, shard_len
    )
    grad_gate = (carried_home * values_wide).astype(jnp.bfloat16)[None]
    grad_values = (carried_home * gate_wide).astype(jnp.bfloat16)[None]
    return (grad_gate, grad_values, grad_filter)


def pack_body(groups, peers, own_ref, gate_ref, values_ref, grad_ref, taps_ref, out_ref):
    part = out_ref.shape[1] // (2 * groups + 2)
    half = groups * part
    for q in range(groups):
        rows = pl.ds(q * peers * part, peers * part)
        mixed = gate_ref[rows, :].astype(jnp.float32) * values_ref[rows, :].astype(jnp.float32)
        out_ref[:, q * part : (q + 1) * part, :] = grad_ref[rows, :].reshape(peers, part, LANES)
        out_ref[:, half + q * part : half + (q + 1) * part, :] = mixed.astype(jnp.bfloat16).reshape(
            peers, part, LANES
        )
    first = pl.multiple_of(own_ref[0] * (peers * part), peers * part)
    taps = taps_ref[pl.ds(first, peers * part), :]
    high = taps.astype(jnp.bfloat16)
    low = (taps - high.astype(jnp.float32)).astype(jnp.bfloat16)
    out_ref[:, 2 * half : 2 * half + part, :] = high.reshape(peers, part, LANES)
    out_ref[:, 2 * half + part :, :] = low.reshape(peers, part, LANES)


def correlate_body(seqs, blocks, unroll, in_ref, out_ref, gs, ms, fs, cs, rs, pads, hs, ts):
    peers = seqs * blocks
    part = in_ref.shape[1] // (2 * seqs + 2)
    held = seqs * part
    steps = LANES // REACH
    near = lax.broadcasted_iota(jnp.int32, (REACH, LANES), 0)
    lane = lax.broadcasted_iota(jnp.int32, (REACH, LANES), 1)
    flip = jnp.where(lane % REACH + near == REACH - 1, 1.0, 0.0).astype(jnp.bfloat16)
    ours = lax.broadcasted_iota(jnp.int32, (peers, LANES), 1) // REACH
    inside = lane + REACH - 1 - near < LANES
    ahead = lane >= near
    thin = lax.broadcasted_iota(jnp.int32, (blocks, LANES), 1)
    across = (((1,), (1,)), ((), ()))
    span = blocks * held
    for b in range(seqs):
        mine = slice(b * blocks, (b + 1) * blocks)
        gs[pl.ds(b * span, span), :] = (
            in_ref[mine, :held, :].astype(jnp.float32).reshape(span, LANES)
        )
        ms[pl.ds(b * span, span), :] = (
            in_ref[mine, held : 2 * held, :].astype(jnp.float32).reshape(span, LANES)
        )
        for s in range(blocks):
            high = in_ref[b * blocks + s, 2 * held : 2 * held + part, :].astype(jnp.float32)
            low = in_ref[b * blocks + s, 2 * held + part :, :].astype(jnp.float32)
            fs[pl.ds(s * held + b * part, part), :] = high + low
    pads[...] = jnp.zeros_like(pads)

    def at(u, q, b):
        return ((u * steps + q) * seqs + b) * 2 * blocks

    def several(i, carry):
        lot = [(u, i * unroll + u) for u in range(unroll)]
        for u, c in lot:
            for b in range(seqs):
                pads[pl.ds(at(u, 0, b), blocks), :] = gs[pl.ds(b * span + c, blocks, stride=held), :]
        turned = []
        for u, c in lot:
            mixed = ms[pl.ds(c, peers, stride=held), :]
            mixed = jnp.concatenate(
                [jnp.where(ours == q, mixed, 0.0).astype(jnp.bfloat16) for q in range(steps)], axis=0
            )
            turned.append(
                lax.dot_general(flip, mixed, across, preferred_element_type=jnp.float32).astype(
                    jnp.bfloat16
                )
            )
        for u, c in lot:
            for q in range(1, steps):
                for b in range(seqs):
                    here = pads[pl.ds(at(u, 0, b), blocks), :]
                    then = pads[pl.ds(at(u, 0, b) + 1, blocks), :]
                    pads[pl.ds(at(u, q, b), blocks), :] = pltpu.roll(
                        jnp.where(thin >= q * REACH, here, then), LANES - q * REACH, 1
                    )
        for u, c in lot:
            taps = fs[pl.ds(c, blocks, stride=held), :]
            before = jnp.zeros((REACH, LANES), jnp.float32)
            for k in range(blocks):
                turn = pltpu.roll(
                    jnp.broadcast_to(taps[k : k + 1, :], (REACH, LANES)),
                    0,
                    1,
                    stride=1,
                    stride_axis=0,
                )
                block = jnp.where(ahead, turn, before)
                before = turn
                top = block.astype(jnp.bfloat16)
                ts[u, :REACH, k * LANES : (k + 1) * LANES] = top
                ts[u, REACH:, k * LANES : (k + 1) * LANES] = (
                    block - top.astype(jnp.float32)
                ).astype(jnp.bfloat16)
        for u, c in lot:
            for q in range(steps):
                for k in range(blocks):
                    hs[u, q * peers : (q + 1) * peers, k * LANES : (k + 1) * LANES] = jnp.concatenate(
                        [pads[pl.ds(at(u, q, b) + k, blocks), :] for b in range(seqs)], axis=0
                    ).astype(jnp.bfloat16)
        for u, c in lot:
            gram = jnp.dot(turned[u], hs[u], preferred_element_type=jnp.float32)
            later = jnp.zeros((REACH, LANES), jnp.float32)
            sums = []
            for k in reversed(range(blocks)):
                turn = pltpu.roll(
                    gram[:, k * LANES : (k + 1) * LANES],
                    LANES + 1 - REACH,
                    1,
                    stride=1,
                    stride_axis=0,
                )
                sums.append(jnp.sum(jnp.where(inside, turn, later), axis=0, keepdims=True))
                later = turn
            rs[pl.ds(c, blocks, stride=held), :] = jnp.concatenate(sums[::-1], axis=0)
        for u, c in lot:
            short = lax.dot_general(hs[u], ts[u], across, preferred_element_type=jnp.float32)
            short = jnp.concatenate(
                [short, jnp.zeros((steps * peers, LANES - 2 * REACH), jnp.float32)], axis=1
            )
            carried = None
            for q in range(steps):
                mine = short[q * peers : (q + 1) * peers]
                both = pltpu.roll(mine, q * REACH, 1) if q else mine
                back = (q - 1) % steps
                both = both + (pltpu.roll(mine, back * REACH, 1) if back else mine)
                carried = both if carried is None else jnp.where(ours == q, both, carried)
            cs[pl.ds(c, peers, stride=held), :] = carried
        return carry

    lax.fori_loop(0, held // unroll, several, 0)
    out_ref[:, :held, :] = cs[...].reshape(peers, held, LANES).astype(jnp.bfloat16)
    for q in range(seqs):
        for s in range(blocks):
            out_ref[q * blocks + s, held:, :] = rs[pl.ds(s * held + q * part, part), :].astype(
                jnp.bfloat16
            )


def unpack_body(groups, in_ref, gate_ref, values_ref, gate_out, values_out, filter_out):
    peers = in_ref.shape[0]
    part = in_ref.shape[1] // (groups + 1)
    for q in range(groups):
        rows = pl.ds(q * peers * part, peers * part)
        carried = (
            in_ref[:, q * part : (q + 1) * part, :].astype(jnp.float32).reshape(peers * part, LANES)
        )
        gate_out[rows, :] = (carried * values_ref[rows, :].astype(jnp.float32)).astype(jnp.bfloat16)
        values_out[rows, :] = (carried * gate_ref[rows, :].astype(jnp.float32)).astype(jnp.bfloat16)
    filter_out[...] = (
        in_ref[:, groups * part :, :].astype(jnp.float32).reshape(peers * part, LANES)
    )


def correlate(arrived, seqs):
    peers, rows, _ = arrived.shape
    blocks = peers // seqs
    part = rows // (2 * seqs + 2)
    held = seqs * part
    whole = pl.BlockSpec(memory_space=pltpu.VMEM)
    return pl.pallas_call(
        functools.partial(correlate_body, seqs, blocks, UNROLL),
        out_shape=jax.ShapeDtypeStruct((peers, held + part, LANES), jnp.bfloat16),
        in_specs=[whole],
        out_specs=whole,
        scratch_shapes=[
            pltpu.VMEM((peers * held, LANES), jnp.float32),
            pltpu.VMEM((peers * held, LANES), jnp.float32),
            pltpu.VMEM((blocks * held, LANES), jnp.float32),
            pltpu.VMEM((peers * held, LANES), jnp.float32),
            pltpu.VMEM((blocks * held, LANES), jnp.float32),
            pltpu.VMEM((UNROLL * (LANES // REACH) * 2 * peers, LANES), jnp.float32),
            pltpu.VMEM((UNROLL, LANES // REACH * peers, blocks * LANES), jnp.bfloat16),
            pltpu.VMEM((UNROLL, 2 * REACH, blocks * LANES), jnp.bfloat16),
        ],
        cost_estimate=pl.CostEstimate(
            flops=6 * held * LANES * blocks * LANES * peers, bytes_accessed=4 * arrived.size, transcendentals=0
        ),
    )(arrived)


def direct_shards(gate_in, values_in, out_grad, filter_taps):
    groups = lax.axis_size("dp")
    peers = groups * lax.axis_size("seq")
    channels = gate_in.shape[1]
    part = channels // (groups * peers)
    whole = pl.BlockSpec(memory_space=pltpu.VMEM)
    own = lax.axis_index("dp").astype(jnp.int32).reshape(1)
    packed = pl.pallas_call(
        functools.partial(pack_body, groups, peers),
        out_shape=jax.ShapeDtypeStruct((peers, (2 * groups + 2) * part, LANES), jnp.bfloat16),
        in_specs=[pl.BlockSpec(memory_space=pltpu.SMEM), whole, whole, whole, whole],
        out_specs=whole,
    )(own, gate_in[0], values_in[0], out_grad[0], filter_taps)
    arrived = lax.all_to_all(packed, ("dp", "seq"), split_axis=0, concat_axis=0, tiled=True)
    made = correlate(arrived, groups)
    home = lax.all_to_all(made, ("dp", "seq"), split_axis=0, concat_axis=0, tiled=True)
    wide = jax.ShapeDtypeStruct((channels, LANES), jnp.bfloat16)
    grad_gate, grad_values, grad_filter = pl.pallas_call(
        functools.partial(unpack_body, groups),
        out_shape=(wide, wide, jax.ShapeDtypeStruct((channels // groups, LANES), jnp.float32)),
        in_specs=[whole, whole, whole],
        out_specs=(whole, whole, whole),
    )(home, gate_in[0], values_in[0])
    return (grad_gate[None], grad_values[None], grad_filter)


def shards(gate_in, values_in, out_grad, filter_taps):
    groups = lax.axis_size("dp")
    peers = groups * lax.axis_size("seq")
    channels, shard_len = gate_in.shape[1:]
    part = channels // (groups * peers)
    fits = 24 * channels * LANES * groups <= ROOM
    if shard_len == LANES and channels == part * groups * peers and part % SUBLANES == 0 and fits:
        return direct_shards(gate_in, values_in, out_grad, filter_taps)
    return spectral_shards(gate_in, values_in, out_grad, filter_taps)


def solution(mesh):
    return jax.shard_map(
        shards,
        mesh=mesh,
        in_specs=(P("dp", None, "seq"), P("dp", None, "seq"), P("dp", None, "seq"), P(None, "seq")),
        out_specs=(P("dp", None, "seq"), P("dp", None, "seq"), P("dp", "seq")),
        check_vma=False,
    )
```

```python
import functools
import math

import jax
import jax.numpy as jnp
from jax import lax
from jax.experimental import pallas as pl
from jax.experimental.pallas import tpu as pltpu
from jax.sharding import PartitionSpec as P

LANES = 128
SUBLANES = 16
REACH = 32
UNROLL = 8
ROOM = 40 * 2**20

precise = lax.Precision.HIGHEST
coarse = lax.Precision.HIGH


def spin_tables(count_in, count_out, period):
    rows = lax.broadcasted_iota(jnp.int32, (count_in, count_out), 0)
    cols = lax.broadcasted_iota(jnp.int32, (count_in, count_out), 1)
    phase = (rows * cols % period).astype(jnp.float32) * (2.0 * math.pi / period)
    return (jnp.cos(phase), jnp.sin(phase))


def make_tables(length, columns):
    rows_in = length // columns
    rows_out = 2 * rows_in
    first_cos, first_sin = spin_tables(rows_in, rows_out, rows_out)
    turn = spin_tables(rows_out, columns, 2 * length)
    last_cos, last_sin = spin_tables(columns, columns, columns)
    first_fwd = jnp.concatenate([first_cos, -first_sin], axis=1)
    last_fwd = jnp.concatenate(
        [
            jnp.concatenate([last_cos, -last_sin], axis=1),
            jnp.concatenate([last_sin, last_cos], axis=1),
        ],
        axis=0,
    )
    last_inv = jnp.concatenate(
        [
            jnp.concatenate([last_cos.T, last_sin.T], axis=1),
            jnp.concatenate([-last_sin.T, last_cos.T], axis=1),
        ],
        axis=0,
    )
    first_inv = jnp.concatenate(
        [
            jnp.concatenate([first_cos.T, first_sin.T], axis=1),
            jnp.concatenate([-first_sin.T, first_cos.T], axis=1),
        ],
        axis=0,
    )
    return (first_fwd, turn, last_fwd, last_inv, first_inv)


def spectrum(signal, tables, columns, first_precision):
    first_fwd, (turn_cos, turn_sin), last_fwd, last_inv, first_inv = tables
    held, length = signal.shape
    half = turn_cos.shape[0]
    grid = signal.reshape(held, length // columns, columns)
    part = jnp.einsum("cmn,mk->ckn", grid, first_fwd, precision=first_precision)
    part_real = part[:, :half]
    part_imag = part[:, half:]
    turned = jnp.concatenate(
        [part_real * turn_cos + part_imag * turn_sin, part_imag * turn_cos - part_real * turn_sin],
        axis=2,
    )
    out = jnp.einsum("ckn,nj->ckj", turned, last_fwd, precision=first_precision)
    return (out[:, :, :columns], out[:, :, columns:])


def to_signal(spec_real, spec_imag, tables, length):
    first_fwd, (turn_cos, turn_sin), last_fwd, last_inv, first_inv = tables
    held = spec_real.shape[0]
    columns = spec_real.shape[2]
    rows_in = length // columns
    stacked = jnp.concatenate([spec_real, spec_imag], axis=2)
    back = jnp.einsum("ckj,jn->ckn", stacked, last_inv, precision=coarse)
    back_real = back[:, :, :columns]
    back_imag = back[:, :, columns:]
    turned = jnp.concatenate(
        [back_real * turn_cos - back_imag * turn_sin, back_imag * turn_cos + back_real * turn_sin],
        axis=1,
    )
    factor = 1.0 / (2 * length)
    both = jnp.einsum("ckn,km->cmn", turned, first_inv, precision=coarse) * factor
    real_part = both[:, :rows_in]
    imag_part = both[:, rows_in:]
    return (real_part.reshape(held, length), imag_part.reshape(held, length))


def spectral_shards(gate_in, values_in, out_grad, filter_taps):
    seq_count = lax.axis_size("seq")
    group_count = lax.axis_size("dp")
    channels = gate_in.shape[1]
    shard_len = gate_in.shape[2]
    length = shard_len * seq_count
    quarter = channels // group_count
    per_block = quarter // seq_count
    held_channels = group_count * per_block
    columns = 128 if length % 128 == 0 and length >= 8192 else 32
    tables = make_tables(length, columns)
    gate_wide = gate_in[0].astype(jnp.float32)
    values_wide = values_in[0].astype(jnp.float32)
    mixed = (gate_wide * values_wide).astype(jnp.bfloat16)
    grad_rows, mixed_rows = (
        lax.all_to_all(
            out_grad[0].reshape(group_count, quarter, shard_len),
            "seq",
            split_axis=1,
            concat_axis=2,
            tiled=True,
        ),
        lax.all_to_all(
            mixed.reshape(group_count, quarter, shard_len),
            "seq",
            split_axis=1,
            concat_axis=2,
            tiled=True,
        ),
    )
    filter_grouped = filter_taps.reshape(group_count, quarter, shard_len)
    filter_rows = lax.all_to_all(filter_grouped, "seq", split_axis=1, concat_axis=2, tiled=True)
    grad_real, grad_imag = spectrum(
        grad_rows.reshape(held_channels, length).astype(jnp.float32), tables, columns, coarse
    )
    mix_real, mix_imag = spectrum(
        mixed_rows.reshape(held_channels, length).astype(jnp.float32), tables, columns, coarse
    )
    tap_real, tap_imag = spectrum(
        filter_rows.reshape(held_channels, length), tables, columns, precise
    )
    carry_real = tap_real * grad_real + tap_imag * grad_imag
    carry_imag = tap_real * grad_imag - tap_imag * grad_real
    lag_real = grad_real * mix_real + grad_imag * mix_imag
    lag_imag = grad_imag * mix_real - grad_real * mix_imag
    carried, lagged = to_signal(carry_real - lag_imag, carry_imag + lag_real, tables, length)
    carried = carried.astype(jnp.bfloat16).reshape(group_count, per_block, length)
    returned = lax.all_to_all(carried, "seq", split_axis=2, concat_axis=1, tiled=True)
    carried_home = returned.reshape(channels, shard_len).astype(jnp.float32)
    lagged = lagged.reshape(group_count, per_block, length)
    summed = lax.psum_scatter(lagged, "dp", scatter_dimension=0, tiled=True)
    grad_filter = lax.all_to_all(summed, "seq", split_axis=2, concat_axis=1, tiled=True).reshape(
        quarter, shard_len
    )
    grad_gate = (carried_home * values_wide).astype(jnp.bfloat16)[None]
    grad_values = (carried_home * gate_wide).astype(jnp.bfloat16)[None]
    return (grad_gate, grad_values, grad_filter)


def pack_body(groups, peers, first, count, own_ref, gate_ref, values_ref, grad_ref, taps_ref, out_ref):
    part = gate_ref.shape[0] // (groups * peers)
    half = count * part
    for i in range(count):
        rows = pl.ds((first + i) * peers * part, peers * part)
        mixed = gate_ref[rows, :].astype(jnp.float32) * values_ref[rows, :].astype(jnp.float32)
        out_ref[:, i * part : (i + 1) * part, :] = grad_ref[rows, :].reshape(peers, part, LANES)
        out_ref[:, half + i * part : half + (i + 1) * part, :] = mixed.astype(jnp.bfloat16).reshape(
            peers, part, LANES
        )
    if not first:
        start = pl.multiple_of(own_ref[0] * (peers * part), peers * part)
        taps = taps_ref[pl.ds(start, peers * part), :]
        high = taps.astype(jnp.bfloat16)
        low = (taps - high.astype(jnp.float32)).astype(jnp.bfloat16)
        out_ref[:, 2 * half : 2 * half + part, :] = high.reshape(peers, part, LANES)
        out_ref[:, 2 * half + part :, :] = low.reshape(peers, part, LANES)


def correlate_body(
    seqs, blocks, unroll, part, first, count, *refs
):
    peers = seqs * blocks
    held = count * part
    in_ref, taps_ref, *refs = refs
    past_ref = None
    if first:
        past_ref, *refs = refs
        out_ref, *refs = refs
    else:
        out_ref, sum_ref, *refs = refs
    gs, ms, fs, cs, rs, pads, hs, ts = refs
    steps = LANES // REACH
    near = lax.broadcasted_iota(jnp.int32, (REACH, LANES), 0)
    lane = lax.broadcasted_iota(jnp.int32, (REACH, LANES), 1)
    flip = jnp.where(lane % REACH + near == REACH - 1, 1.0, 0.0).astype(jnp.bfloat16)
    ours = lax.broadcasted_iota(jnp.int32, (peers, LANES), 1) // REACH
    inside = lane + REACH - 1 - near < LANES
    ahead = lane >= near
    thin = lax.broadcasted_iota(jnp.int32, (blocks, LANES), 1)
    across = (((1,), (1,)), ((), ()))
    span = blocks * held
    for b in range(seqs):
        mine = slice(b * blocks, (b + 1) * blocks)
        gs[pl.ds(b * span, span), :] = (
            in_ref[mine, :held, :].astype(jnp.float32).reshape(span, LANES)
        )
        ms[pl.ds(b * span, span), :] = (
            in_ref[mine, held : 2 * held, :].astype(jnp.float32).reshape(span, LANES)
        )
    base = taps_ref.shape[1] - 2 * part
    for i in range(count):
        for s in range(blocks):
            p = (first + i) * blocks + s
            high = taps_ref[p, base : base + part, :].astype(jnp.float32)
            low = taps_ref[p, base + part :, :].astype(jnp.float32)
            fs[pl.ds(s * held + i * part, part), :] = high + low
    pads[...] = jnp.zeros_like(pads)

    def at(u, q, b):
        return ((u * steps + q) * seqs + b) * 2 * blocks

    def several(i, carry):
        lot = [(u, i * unroll + u) for u in range(unroll)]
        for u, c in lot:
            for b in range(seqs):
                pads[pl.ds(at(u, 0, b), blocks), :] = gs[pl.ds(b * span + c, blocks, stride=held), :]
        turned = []
        for u, c in lot:
            mixed = ms[pl.ds(c, peers, stride=held), :]
            mixed = jnp.concatenate(
                [jnp.where(ours == q, mixed, 0.0).astype(jnp.bfloat16) for q in range(steps)], axis=0
            )
            turned.append(
                lax.dot_general(flip, mixed, across, preferred_element_type=jnp.float32).astype(
                    jnp.bfloat16
                )
            )
        for u, c in lot:
            for q in range(1, steps):
                for b in range(seqs):
                    here = pads[pl.ds(at(u, 0, b), blocks), :]
                    then = pads[pl.ds(at(u, 0, b) + 1, blocks), :]
                    pads[pl.ds(at(u, q, b), blocks), :] = pltpu.roll(
                        jnp.where(thin >= q * REACH, here, then), LANES - q * REACH, 1
                    )
        for u, c in lot:
            taps = fs[pl.ds(c, blocks, stride=held), :]
            before = jnp.zeros((REACH, LANES), jnp.float32)
            for k in range(blocks):
                turn = pltpu.roll(
                    jnp.broadcast_to(taps[k : k + 1, :], (REACH, LANES)),
                    0,
                    1,
                    stride=1,
                    stride_axis=0,
                )
                block = jnp.where(ahead, turn, before)
                before = turn
                top = block.astype(jnp.bfloat16)
                ts[u, :REACH, k * LANES : (k + 1) * LANES] = top
                ts[u, REACH:, k * LANES : (k + 1) * LANES] = (
                    block - top.astype(jnp.float32)
                ).astype(jnp.bfloat16)
        for u, c in lot:
            for q in range(steps):
                for k in range(blocks):
                    hs[u, q * peers : (q + 1) * peers, k * LANES : (k + 1) * LANES] = jnp.concatenate(
                        [pads[pl.ds(at(u, q, b) + k, blocks), :] for b in range(seqs)], axis=0
                    ).astype(jnp.bfloat16)
        for u, c in lot:
            gram = jnp.dot(turned[u], hs[u], preferred_element_type=jnp.float32)
            later = jnp.zeros((REACH, LANES), jnp.float32)
            sums = []
            for k in reversed(range(blocks)):
                turn = pltpu.roll(
                    gram[:, k * LANES : (k + 1) * LANES],
                    LANES + 1 - REACH,
                    1,
                    stride=1,
                    stride_axis=0,
                )
                sums.append(jnp.sum(jnp.where(inside, turn, later), axis=0, keepdims=True))
                later = turn
            rs[pl.ds(c, blocks, stride=held), :] = jnp.concatenate(sums[::-1], axis=0)
        for u, c in lot:
            short = lax.dot_general(hs[u], ts[u], across, preferred_element_type=jnp.float32)
            short = jnp.concatenate(
                [short, jnp.zeros((steps * peers, LANES - 2 * REACH), jnp.float32)], axis=1
            )
            carried = None
            for q in range(steps):
                mine = short[q * peers : (q + 1) * peers]
                both = pltpu.roll(mine, q * REACH, 1) if q else mine
                back = (q - 1) % steps
                both = both + (pltpu.roll(mine, back * REACH, 1) if back else mine)
                carried = both if carried is None else jnp.where(ours == q, both, carried)
            cs[pl.ds(c, peers, stride=held), :] = carried
        return carry

    lax.fori_loop(0, held // unroll, several, 0)
    out_ref[:, :held, :] = cs[...].reshape(peers, held, LANES).astype(jnp.bfloat16)
    if first:
        out_ref[: first * blocks, held:, :] = past_ref[...]
    for i in range(count):
        for s in range(blocks):
            block = rs[pl.ds(s * held + i * part, part), :].astype(jnp.bfloat16)
            if first:
                out_ref[(first + i) * blocks + s, held:, :] = block
            else:
                sum_ref[i * blocks + s] = block


def unpack_body(groups, early_ref, late_ref, gate_ref, values_ref, gate_out, values_out, filter_out):
    peers = early_ref.shape[0]
    part = gate_ref.shape[0] // (groups * peers)
    count = early_ref.shape[1] // part
    for q in range(groups):
        rows = pl.ds(q * peers * part, peers * part)
        src, i = (early_ref, q) if q < count else (late_ref, q - count)
        carried = src[:, i * part : (i + 1) * part, :].astype(jnp.float32)
        carried = carried.reshape(peers * part, LANES)
        gate_out[rows, :] = (carried * values_ref[rows, :].astype(jnp.float32)).astype(jnp.bfloat16)
        values_out[rows, :] = (carried * gate_ref[rows, :].astype(jnp.float32)).astype(jnp.bfloat16)
    filter_out[...] = (
        late_ref[:, (groups - count) * part :, :].astype(jnp.float32).reshape(peers * part, LANES)
    )


def correlate(seqs, part, first, count, *arrays):
    peers = arrays[0].shape[0]
    blocks = peers // seqs
    held = count * part
    whole = pl.BlockSpec(memory_space=pltpu.VMEM)
    if first:
        out_shape = jax.ShapeDtypeStruct((peers, held + part, LANES), jnp.bfloat16)
        out_specs = whole
    else:
        out_shape = (
            jax.ShapeDtypeStruct((peers, held, LANES), jnp.bfloat16),
            jax.ShapeDtypeStruct((count * blocks, part, LANES), jnp.bfloat16),
        )
        out_specs = (whole, whole)
    return pl.pallas_call(
        functools.partial(correlate_body, seqs, blocks, UNROLL, part, first, count),
        out_shape=out_shape,
        in_specs=[whole] * len(arrays),
        out_specs=out_specs,
        scratch_shapes=[
            pltpu.VMEM((peers * held, LANES), jnp.float32),
            pltpu.VMEM((peers * held, LANES), jnp.float32),
            pltpu.VMEM((blocks * held, LANES), jnp.float32),
            pltpu.VMEM((peers * held, LANES), jnp.float32),
            pltpu.VMEM((blocks * held, LANES), jnp.float32),
            pltpu.VMEM((UNROLL * (LANES // REACH) * 2 * peers, LANES), jnp.float32),
            pltpu.VMEM((UNROLL, LANES // REACH * peers, blocks * LANES), jnp.bfloat16),
            pltpu.VMEM((UNROLL, 2 * REACH, blocks * LANES), jnp.bfloat16),
        ],
        cost_estimate=pl.CostEstimate(
            flops=60 * held * LANES * blocks * LANES * peers,
            bytes_accessed=4 * arrays[0].size,
            transcendentals=0,
        ),
    )(*arrays)


def exchange(array):
    return lax.all_to_all(array, ("dp", "seq"), split_axis=0, concat_axis=0, tiled=True)


def direct_shards(gate_in, values_in, out_grad, filter_taps):
    groups = lax.axis_size("dp")
    peers = groups * lax.axis_size("seq")
    channels = gate_in.shape[1]
    part = channels // (groups * peers)
    half = groups // 2
    whole = pl.BlockSpec(memory_space=pltpu.VMEM)
    own = lax.axis_index("dp").astype(jnp.int32).reshape(1)

    def pack(first, count):
        rows = 2 * count + (0 if first else 2)
        return pl.pallas_call(
            functools.partial(pack_body, groups, peers, first, count),
            out_shape=jax.ShapeDtypeStruct((peers, rows * part, LANES), jnp.bfloat16),
            in_specs=[pl.BlockSpec(memory_space=pltpu.SMEM), whole, whole, whole, whole],
            out_specs=whole,
        )(own, gate_in[0], values_in[0], out_grad[0], filter_taps)

    early = exchange(pack(0, half))
    late = exchange(pack(half, groups - half))
    made, sums = correlate(groups, part, 0, half, early, early)
    early_home = exchange(made)
    made = correlate(groups, part, half, groups - half, late, early, sums)
    late_home = exchange(made)
    wide = jax.ShapeDtypeStruct((channels, LANES), jnp.bfloat16)
    grad_gate, grad_values, grad_filter = pl.pallas_call(
        functools.partial(unpack_body, groups),
        out_shape=(wide, wide, jax.ShapeDtypeStruct((channels // groups, LANES), jnp.float32)),
        in_specs=[whole] * 4,
        out_specs=(whole, whole, whole),
    )(early_home, late_home, gate_in[0], values_in[0])
    return (grad_gate[None], grad_values[None], grad_filter)


def shards(gate_in, values_in, out_grad, filter_taps):
    groups = lax.axis_size("dp")
    peers = groups * lax.axis_size("seq")
    channels, shard_len = gate_in.shape[1:]
    part = channels // (groups * peers)
    fits = 24 * channels * LANES * groups <= ROOM
    if shard_len == LANES and channels == part * groups * peers and part % SUBLANES == 0 and fits:
        return direct_shards(gate_in, values_in, out_grad, filter_taps)
    return spectral_shards(gate_in, values_in, out_grad, filter_taps)


def solution(mesh):
    return jax.shard_map(
        shards,
        mesh=mesh,
        in_specs=(P("dp", None, "seq"), P("dp", None, "seq"), P("dp", None, "seq"), P(None, "seq")),
        out_specs=(P("dp", None, "seq"), P("dp", None, "seq"), P("dp", "seq")),
        check_vma=False,
    )
```

```python
import functools
import math

import jax
import jax.numpy as jnp
from jax import lax
from jax.experimental import pallas as pl
from jax.experimental.pallas import tpu as pltpu
from jax.sharding import PartitionSpec as P

LANES = 128
SUBLANES = 16
REACH = 32
UNROLL = 8
ROOM = 40 * 2**20

precise = lax.Precision.HIGHEST
coarse = lax.Precision.HIGH


def spin_tables(count_in, count_out, period):
    rows = lax.broadcasted_iota(jnp.int32, (count_in, count_out), 0)
    cols = lax.broadcasted_iota(jnp.int32, (count_in, count_out), 1)
    phase = (rows * cols % period).astype(jnp.float32) * (2.0 * math.pi / period)
    return (jnp.cos(phase), jnp.sin(phase))


def make_tables(length, columns):
    rows_in = length // columns
    rows_out = 2 * rows_in
    first_cos, first_sin = spin_tables(rows_in, rows_out, rows_out)
    turn = spin_tables(rows_out, columns, 2 * length)
    last_cos, last_sin = spin_tables(columns, columns, columns)
    first_fwd = jnp.concatenate([first_cos, -first_sin], axis=1)
    last_fwd = jnp.concatenate(
        [
            jnp.concatenate([last_cos, -last_sin], axis=1),
            jnp.concatenate([last_sin, last_cos], axis=1),
        ],
        axis=0,
    )
    last_inv = jnp.concatenate(
        [
            jnp.concatenate([last_cos.T, last_sin.T], axis=1),
            jnp.concatenate([-last_sin.T, last_cos.T], axis=1),
        ],
        axis=0,
    )
    first_inv = jnp.concatenate(
        [
            jnp.concatenate([first_cos.T, first_sin.T], axis=1),
            jnp.concatenate([-first_sin.T, first_cos.T], axis=1),
        ],
        axis=0,
    )
    return (first_fwd, turn, last_fwd, last_inv, first_inv)


def spectrum(signal, tables, columns, first_precision):
    first_fwd, (turn_cos, turn_sin), last_fwd, last_inv, first_inv = tables
    held, length = signal.shape
    half = turn_cos.shape[0]
    grid = signal.reshape(held, length // columns, columns)
    part = jnp.einsum("cmn,mk->ckn", grid, first_fwd, precision=first_precision)
    part_real = part[:, :half]
    part_imag = part[:, half:]
    turned = jnp.concatenate(
        [part_real * turn_cos + part_imag * turn_sin, part_imag * turn_cos - part_real * turn_sin],
        axis=2,
    )
    out = jnp.einsum("ckn,nj->ckj", turned, last_fwd, precision=first_precision)
    return (out[:, :, :columns], out[:, :, columns:])


def to_signal(spec_real, spec_imag, tables, length):
    first_fwd, (turn_cos, turn_sin), last_fwd, last_inv, first_inv = tables
    held = spec_real.shape[0]
    columns = spec_real.shape[2]
    rows_in = length // columns
    stacked = jnp.concatenate([spec_real, spec_imag], axis=2)
    back = jnp.einsum("ckj,jn->ckn", stacked, last_inv, precision=coarse)
    back_real = back[:, :, :columns]
    back_imag = back[:, :, columns:]
    turned = jnp.concatenate(
        [back_real * turn_cos - back_imag * turn_sin, back_imag * turn_cos + back_real * turn_sin],
        axis=1,
    )
    factor = 1.0 / (2 * length)
    both = jnp.einsum("ckn,km->cmn", turned, first_inv, precision=coarse) * factor
    real_part = both[:, :rows_in]
    imag_part = both[:, rows_in:]
    return (real_part.reshape(held, length), imag_part.reshape(held, length))


def spectral_shards(gate_in, values_in, out_grad, filter_taps):
    seq_count = lax.axis_size("seq")
    group_count = lax.axis_size("dp")
    channels = gate_in.shape[1]
    shard_len = gate_in.shape[2]
    length = shard_len * seq_count
    quarter = channels // group_count
    per_block = quarter // seq_count
    held_channels = group_count * per_block
    columns = 128 if length % 128 == 0 and length >= 8192 else 32
    tables = make_tables(length, columns)
    gate_wide = gate_in[0].astype(jnp.float32)
    values_wide = values_in[0].astype(jnp.float32)
    mixed = (gate_wide * values_wide).astype(jnp.bfloat16)
    grad_rows, mixed_rows = (
        lax.all_to_all(
            out_grad[0].reshape(group_count, quarter, shard_len),
            "seq",
            split_axis=1,
            concat_axis=2,
            tiled=True,
        ),
        lax.all_to_all(
            mixed.reshape(group_count, quarter, shard_len),
            "seq",
            split_axis=1,
            concat_axis=2,
            tiled=True,
        ),
    )
    filter_grouped = filter_taps.reshape(group_count, quarter, shard_len)
    filter_rows = lax.all_to_all(filter_grouped, "seq", split_axis=1, concat_axis=2, tiled=True)
    grad_real, grad_imag = spectrum(
        grad_rows.reshape(held_channels, length).astype(jnp.float32), tables, columns, coarse
    )
    mix_real, mix_imag = spectrum(
        mixed_rows.reshape(held_channels, length).astype(jnp.float32), tables, columns, coarse
    )
    tap_real, tap_imag = spectrum(
        filter_rows.reshape(held_channels, length), tables, columns, precise
    )
    carry_real = tap_real * grad_real + tap_imag * grad_imag
    carry_imag = tap_real * grad_imag - tap_imag * grad_real
    lag_real = grad_real * mix_real + grad_imag * mix_imag
    lag_imag = grad_imag * mix_real - grad_real * mix_imag
    carried, lagged = to_signal(carry_real - lag_imag, carry_imag + lag_real, tables, length)
    carried = carried.astype(jnp.bfloat16).reshape(group_count, per_block, length)
    returned = lax.all_to_all(carried, "seq", split_axis=2, concat_axis=1, tiled=True)
    carried_home = returned.reshape(channels, shard_len).astype(jnp.float32)
    lagged = lagged.reshape(group_count, per_block, length)
    summed = lax.psum_scatter(lagged, "dp", scatter_dimension=0, tiled=True)
    grad_filter = lax.all_to_all(summed, "seq", split_axis=2, concat_axis=1, tiled=True).reshape(
        quarter, shard_len
    )
    grad_gate = (carried_home * values_wide).astype(jnp.bfloat16)[None]
    grad_values = (carried_home * gate_wide).astype(jnp.bfloat16)[None]
    return (grad_gate, grad_values, grad_filter)


def pack_body(
    groups, own_ref, gate_ref, values_ref, grad_ref, taps_ref, out_ref,
    gate, values, grad, taps, mixed, split, in_sems, out_sems,
):
    part = grad.shape[2]

    def sent(buffer, block, sem):
        rows = pl.ds(block * part, part)
        return pltpu.make_async_copy(buffer, out_ref.at[:, rows, :], out_sems.at[sem])

    loads = {}
    for q in range(groups):
        loads["grad", q] = pltpu.make_async_copy(grad_ref.at[q], grad.at[q], in_sems.at[q])
    for q in range(groups):
        loads["gate", q] = pltpu.make_async_copy(
            gate_ref.at[q], gate.at[q], in_sems.at[groups + 2 * q]
        )
        loads["values", q] = pltpu.make_async_copy(
            values_ref.at[q], values.at[q], in_sems.at[groups + 2 * q + 1]
        )
    loads["taps", 0] = pltpu.make_async_copy(
        taps_ref.at[own_ref[0]], taps, in_sems.at[3 * groups]
    )
    for copy in loads.values():
        copy.start()
    sends = []
    for q in range(groups):
        loads["grad", q].wait()
        sends.append(sent(grad.at[q], q, q))
        sends[-1].start()
    for q in range(groups):
        loads["gate", q].wait()
        loads["values", q].wait()
        product = gate[q].astype(jnp.float32) * values[q].astype(jnp.float32)
        mixed[q] = product.astype(jnp.bfloat16)
        sends.append(sent(mixed.at[q], groups + q, groups + q))
        sends[-1].start()
    loads["taps", 0].wait()
    high = taps[...].astype(jnp.bfloat16)
    split[0] = high
    split[1] = (taps[...] - high.astype(jnp.float32)).astype(jnp.bfloat16)
    for i in range(2):
        sends.append(sent(split.at[i], 2 * groups + i, 2 * groups + i))
        sends[-1].start()
    for copy in sends:
        copy.wait()


def correlate_body(seqs, blocks, unroll, in_ref, out_ref, gs, ms, fs, cs, rs, pads, hs0, ts0, tn0, hs1, ts1, tn1):
    peers = seqs * blocks
    part = in_ref.shape[1] // (2 * seqs + 2)
    held = seqs * part
    steps = LANES // REACH
    near = lax.broadcasted_iota(jnp.int32, (REACH, LANES), 0)
    lane = lax.broadcasted_iota(jnp.int32, (REACH, LANES), 1)
    flip = jnp.where(lane % REACH + near == REACH - 1, 1.0, 0.0).astype(jnp.bfloat16)
    ours = lax.broadcasted_iota(jnp.int32, (peers, LANES), 1) // REACH
    inside = lane + REACH - 1 - near < LANES
    ahead = lane >= near
    deep = lax.broadcasted_iota(jnp.int32, (blocks, LANES), 0)
    thin = lax.broadcasted_iota(jnp.int32, (blocks, LANES), 1)
    across = (((1,), (1,)), ((), ()))
    span = blocks * held
    for b in range(seqs):
        mine = slice(b * blocks, (b + 1) * blocks)
        gs[pl.ds(b * span, span), :] = (
            in_ref[mine, :held, :].astype(jnp.float32).reshape(span, LANES)
        )
        ms[pl.ds(b * span, span), :] = (
            in_ref[mine, held : 2 * held, :].astype(jnp.float32).reshape(span, LANES)
        )
        for s in range(blocks):
            high = in_ref[b * blocks + s, 2 * held : 2 * held + part, :].astype(jnp.float32)
            low = in_ref[b * blocks + s, 2 * held + part :, :].astype(jnp.float32)
            fs[pl.ds(s * held + b * part, part), :] = high + low
    pads[...] = jnp.zeros_like(pads)

    def at(u, q, b):
        return ((u * steps + q) * seqs + b) * 2 * blocks

    def turn_over(group, tn):
        for u in range(unroll):
            c = group * unroll + u
            mixed = ms[pl.ds(c, peers, stride=held), :]
            mixed = jnp.concatenate(
                [jnp.where(ours == q, mixed, 0.0).astype(jnp.bfloat16) for q in range(steps)], axis=0
            )
            tn[u] = lax.dot_general(
                flip, mixed, across, preferred_element_type=jnp.float32
            ).astype(jnp.bfloat16)

    def build(group, hs, ts):
        for u in range(unroll):
            c = group * unroll + u
            for b in range(seqs):
                pads[pl.ds(at(u, 0, b), blocks), :] = gs[pl.ds(b * span + c, blocks, stride=held), :]
        for u in range(unroll):
            for q in range(1, steps):
                for b in range(seqs):
                    here = pads[pl.ds(at(u, 0, b), blocks), :]
                    then = pads[pl.ds(at(u, 0, b) + 1, blocks), :]
                    pads[pl.ds(at(u, q, b), blocks), :] = pltpu.roll(
                        jnp.where(thin >= q * REACH, here, then), LANES - q * REACH, 1
                    )
        for u in range(unroll):
            c = group * unroll + u
            taps = fs[pl.ds(c, blocks, stride=held), :]
            before = jnp.zeros((REACH, LANES), jnp.float32)
            for k in range(blocks):
                turn = pltpu.roll(
                    jnp.broadcast_to(taps[k : k + 1, :], (REACH, LANES)),
                    0,
                    1,
                    stride=1,
                    stride_axis=0,
                )
                block = jnp.where(ahead, turn, before)
                before = turn
                top = block.astype(jnp.bfloat16)
                ts[u, k, :REACH, :] = top
                ts[u, k, REACH:, :] = (block - top.astype(jnp.float32)).astype(jnp.bfloat16)
        for u in range(unroll):
            for q in range(steps):
                for k in range(blocks):
                    hs[u, k, q * peers : (q + 1) * peers, :] = jnp.concatenate(
                        [pads[pl.ds(at(u, q, b) + k, blocks), :] for b in range(seqs)], axis=0
                    ).astype(jnp.bfloat16)

    def joined(ref, u):
        return jnp.concatenate([ref[u, k] for k in range(blocks)], axis=1)

    def merged(parts):
        gap = 1
        while len(parts) > 1:
            keep = deep & gap == 0
            parts = [
                jnp.where(keep, x, y) + pltpu.roll(jnp.where(keep, y, x), gap, 0)
                for x, y in zip(parts[0::2], parts[1::2])
            ]
            gap *= 2
        return parts[0]

    def multiply(group, hs, ts, tn):
        for u in range(unroll):
            c = group * unroll + u
            gram = jnp.dot(tn[u], joined(hs, u), preferred_element_type=jnp.float32)
            later = jnp.zeros((REACH, LANES), jnp.float32)
            sums = []
            for k in reversed(range(blocks)):
                turn = pltpu.roll(
                    gram[:, k * LANES : (k + 1) * LANES],
                    LANES + 1 - REACH,
                    1,
                    stride=1,
                    stride_axis=0,
                )
                picked = jnp.where(inside, turn, later)
                sums.append(sum(picked[i : i + blocks] for i in range(0, REACH, blocks)))
                later = turn
            rs[pl.ds(c, blocks, stride=held), :] = merged(sums[::-1])
        for u in range(unroll):
            c = group * unroll + u
            short = lax.dot_general(
                joined(hs, u), joined(ts, u), across, preferred_element_type=jnp.float32
            )
            short = jnp.concatenate(
                [short, jnp.zeros((steps * peers, LANES - 2 * REACH), jnp.float32)], axis=1
            )
            carried = None
            for q in range(steps):
                mine = short[q * peers : (q + 1) * peers]
                both = pltpu.roll(mine, q * REACH, 1) if q else mine
                back = (q - 1) % steps
                both = both + (pltpu.roll(mine, back * REACH, 1) if back else mine)
                carried = both if carried is None else jnp.where(ours == q, both, carried)
            cs[pl.ds(c, peers, stride=held), :] = carried

    total = held // unroll
    turn_over(0, tn0)
    build(0, hs0, ts0)

    def twice(i, carry):
        turn_over(2 * i + 1, tn1)
        multiply(2 * i, hs0, ts0, tn0)
        build(2 * i + 1, hs1, ts1)
        after = jnp.minimum(2 * i + 2, total - 1)
        turn_over(after, tn0)
        multiply(2 * i + 1, hs1, ts1, tn1)
        build(after, hs0, ts0)
        return carry

    lax.fori_loop(0, total // 2, twice, 0)
    out_ref[:, :held, :] = cs[...].reshape(peers, held, LANES).astype(jnp.bfloat16)
    for q in range(seqs):
        for s in range(blocks):
            out_ref[q * blocks + s, held:, :] = rs[pl.ds(s * held + q * part, part), :].astype(
                jnp.bfloat16
            )


def unpack_body(
    groups, in_ref, gate_ref, values_ref, gate_out, values_out, filter_out,
    home, gate, values, gate_made, values_made, sums, in_sems, out_sems,
):
    part = home.shape[2]
    loads, sends = [], []
    for q in range(groups):
        rows = pl.ds(q * part, part)
        loads.append(
            [
                pltpu.make_async_copy(in_ref.at[:, rows, :], home.at[q], in_sems.at[3 * q]),
                pltpu.make_async_copy(gate_ref.at[q], gate.at[q], in_sems.at[3 * q + 1]),
                pltpu.make_async_copy(values_ref.at[q], values.at[q], in_sems.at[3 * q + 2]),
            ]
        )
    tail = pltpu.make_async_copy(
        in_ref.at[:, pl.ds(groups * part, part), :], home.at[groups], in_sems.at[3 * groups]
    )
    for copies in loads:
        for copy in copies:
            copy.start()
    tail.start()
    for q in range(groups):
        for copy in loads[q]:
            copy.wait()
        carried = home[q].astype(jnp.float32)
        gate_made[q] = (carried * values[q].astype(jnp.float32)).astype(jnp.bfloat16)
        values_made[q] = (carried * gate[q].astype(jnp.float32)).astype(jnp.bfloat16)
        for i, (made, out) in enumerate(((gate_made, gate_out), (values_made, values_out))):
            sends.append(pltpu.make_async_copy(made.at[q], out.at[q], out_sems.at[2 * q + i]))
            sends[-1].start()
    tail.wait()
    sums[...] = home[groups].astype(jnp.float32)
    sends.append(pltpu.make_async_copy(sums, filter_out, out_sems.at[2 * groups]))
    sends[-1].start()
    for copy in sends:
        copy.wait()


def correlate(arrived, seqs):
    peers, rows, _ = arrived.shape
    blocks = peers // seqs
    part = rows // (2 * seqs + 2)
    held = seqs * part
    whole = pl.BlockSpec(memory_space=pltpu.VMEM)
    return pl.pallas_call(
        functools.partial(correlate_body, seqs, blocks, UNROLL),
        out_shape=jax.ShapeDtypeStruct((peers, held + part, LANES), jnp.bfloat16),
        in_specs=[whole],
        out_specs=whole,
        scratch_shapes=[
            pltpu.VMEM((peers * held, LANES), jnp.float32),
            pltpu.VMEM((peers * held, LANES), jnp.float32),
            pltpu.VMEM((blocks * held, LANES), jnp.float32),
            pltpu.VMEM((peers * held, LANES), jnp.float32),
            pltpu.VMEM((blocks * held, LANES), jnp.float32),
            pltpu.VMEM((UNROLL * (LANES // REACH) * 2 * peers, LANES), jnp.float32),
            *[
                pltpu.VMEM((UNROLL, blocks, LANES // REACH * peers, LANES), jnp.bfloat16),
                pltpu.VMEM((UNROLL, blocks, 2 * REACH, LANES), jnp.bfloat16),
                pltpu.VMEM((UNROLL, REACH, LANES // REACH * peers), jnp.bfloat16),
            ]
            * 2,
        ],
        cost_estimate=pl.CostEstimate(
            flops=6 * held * LANES * blocks * LANES * peers, bytes_accessed=4 * arrived.size, transcendentals=0
        ),
    )(arrived)


def direct_shards(gate_in, values_in, out_grad, filter_taps):
    groups = lax.axis_size("dp")
    peers = groups * lax.axis_size("seq")
    channels = gate_in.shape[1]
    part = channels // (groups * peers)
    shape = (groups, peers, part, LANES)
    gate, values, grad = (array.reshape(shape) for array in (gate_in, values_in, out_grad))
    taps = filter_taps.reshape(shape)
    own = lax.axis_index("dp").astype(jnp.int32).reshape(1)
    far = pl.BlockSpec(memory_space=pl.ANY)
    half = pltpu.VMEM(shape, jnp.bfloat16)
    packed = pl.pallas_call(
        functools.partial(pack_body, groups),
        out_shape=jax.ShapeDtypeStruct((peers, (2 * groups + 2) * part, LANES), jnp.bfloat16),
        in_specs=[pl.BlockSpec(memory_space=pltpu.SMEM), far, far, far, far],
        out_specs=far,
        scratch_shapes=[
            half,
            half,
            half,
            pltpu.VMEM(shape[1:], jnp.float32),
            half,
            pltpu.VMEM((2,) + shape[1:], jnp.bfloat16),
            pltpu.SemaphoreType.DMA((3 * groups + 1,)),
            pltpu.SemaphoreType.DMA((2 * groups + 2,)),
        ],
    )(own, gate, values, grad, taps)
    arrived = lax.all_to_all(packed, ("dp", "seq"), split_axis=0, concat_axis=0, tiled=True)
    made = correlate(arrived, groups)
    home = lax.all_to_all(made, ("dp", "seq"), split_axis=0, concat_axis=0, tiled=True)
    wide = jax.ShapeDtypeStruct(shape, jnp.bfloat16)
    grad_gate, grad_values, grad_filter = pl.pallas_call(
        functools.partial(unpack_body, groups),
        out_shape=(wide, wide, jax.ShapeDtypeStruct(shape[1:], jnp.float32)),
        in_specs=[far, far, far],
        out_specs=(far, far, far),
        scratch_shapes=[
            pltpu.VMEM((groups + 1,) + shape[1:], jnp.bfloat16),
            half,
            half,
            half,
            half,
            pltpu.VMEM(shape[1:], jnp.float32),
            pltpu.SemaphoreType.DMA((3 * groups + 1,)),
            pltpu.SemaphoreType.DMA((2 * groups + 1,)),
        ],
    )(home, gate, values)
    return (
        grad_gate.reshape(gate_in.shape),
        grad_values.reshape(gate_in.shape),
        grad_filter.reshape(channels // groups, LANES),
    )


def shards(gate_in, values_in, out_grad, filter_taps):
    groups = lax.axis_size("dp")
    peers = groups * lax.axis_size("seq")
    channels, shard_len = gate_in.shape[1:]
    part = channels // (groups * peers)
    fits = 24 * channels * LANES * groups <= ROOM
    if shard_len == LANES and channels == part * groups * peers and part % SUBLANES == 0 and fits:
        return direct_shards(gate_in, values_in, out_grad, filter_taps)
    return spectral_shards(gate_in, values_in, out_grad, filter_taps)


def solution(mesh):
    return jax.shard_map(
        shards,
        mesh=mesh,
        in_specs=(P("dp", None, "seq"), P("dp", None, "seq"), P("dp", None, "seq"), P(None, "seq")),
        out_specs=(P("dp", None, "seq"), P("dp", None, "seq"), P("dp", "seq")),
        check_vma=False,
    )
```

```python
import functools
import math

import jax
import jax.numpy as jnp
from jax import lax
from jax.experimental import pallas as pl
from jax.experimental.pallas import tpu as pltpu
from jax.sharding import PartitionSpec as P

LANES = 128
SUBLANES = 16
REACH = 32
UNROLL = 8
ROOM = 40 * 2**20

precise = lax.Precision.HIGHEST
coarse = lax.Precision.HIGH


def spin_tables(count_in, count_out, period):
    rows = lax.broadcasted_iota(jnp.int32, (count_in, count_out), 0)
    cols = lax.broadcasted_iota(jnp.int32, (count_in, count_out), 1)
    phase = (rows * cols % period).astype(jnp.float32) * (2.0 * math.pi / period)
    return (jnp.cos(phase), jnp.sin(phase))


def make_tables(length, columns):
    rows_in = length // columns
    rows_out = 2 * rows_in
    first_cos, first_sin = spin_tables(rows_in, rows_out, rows_out)
    turn = spin_tables(rows_out, columns, 2 * length)
    last_cos, last_sin = spin_tables(columns, columns, columns)
    first_fwd = jnp.concatenate([first_cos, -first_sin], axis=1)
    last_fwd = jnp.concatenate(
        [
            jnp.concatenate([last_cos, -last_sin], axis=1),
            jnp.concatenate([last_sin, last_cos], axis=1),
        ],
        axis=0,
    )
    last_inv = jnp.concatenate(
        [
            jnp.concatenate([last_cos.T, last_sin.T], axis=1),
            jnp.concatenate([-last_sin.T, last_cos.T], axis=1),
        ],
        axis=0,
    )
    first_inv = jnp.concatenate(
        [
            jnp.concatenate([first_cos.T, first_sin.T], axis=1),
            jnp.concatenate([-first_sin.T, first_cos.T], axis=1),
        ],
        axis=0,
    )
    return (first_fwd, turn, last_fwd, last_inv, first_inv)


def spectrum(signal, tables, columns, first_precision):
    first_fwd, (turn_cos, turn_sin), last_fwd, last_inv, first_inv = tables
    held, length = signal.shape
    half = turn_cos.shape[0]
    grid = signal.reshape(held, length // columns, columns)
    part = jnp.einsum("cmn,mk->ckn", grid, first_fwd, precision=first_precision)
    part_real = part[:, :half]
    part_imag = part[:, half:]
    turned = jnp.concatenate(
        [part_real * turn_cos + part_imag * turn_sin, part_imag * turn_cos - part_real * turn_sin],
        axis=2,
    )
    out = jnp.einsum("ckn,nj->ckj", turned, last_fwd, precision=first_precision)
    return (out[:, :, :columns], out[:, :, columns:])


def to_signal(spec_real, spec_imag, tables, length):
    first_fwd, (turn_cos, turn_sin), last_fwd, last_inv, first_inv = tables
    held = spec_real.shape[0]
    columns = spec_real.shape[2]
    rows_in = length // columns
    stacked = jnp.concatenate([spec_real, spec_imag], axis=2)
    back = jnp.einsum("ckj,jn->ckn", stacked, last_inv, precision=coarse)
    back_real = back[:, :, :columns]
    back_imag = back[:, :, columns:]
    turned = jnp.concatenate(
        [back_real * turn_cos - back_imag * turn_sin, back_imag * turn_cos + back_real * turn_sin],
        axis=1,
    )
    factor = 1.0 / (2 * length)
    both = jnp.einsum("ckn,km->cmn", turned, first_inv, precision=coarse) * factor
    real_part = both[:, :rows_in]
    imag_part = both[:, rows_in:]
    return (real_part.reshape(held, length), imag_part.reshape(held, length))


def spectral_shards(gate_in, values_in, out_grad, filter_taps):
    seq_count = lax.axis_size("seq")
    group_count = lax.axis_size("dp")
    channels = gate_in.shape[1]
    shard_len = gate_in.shape[2]
    length = shard_len * seq_count
    quarter = channels // group_count
    per_block = quarter // seq_count
    held_channels = group_count * per_block
    columns = 128 if length % 128 == 0 and length >= 8192 else 32
    tables = make_tables(length, columns)
    gate_wide = gate_in[0].astype(jnp.float32)
    values_wide = values_in[0].astype(jnp.float32)
    mixed = (gate_wide * values_wide).astype(jnp.bfloat16)
    grad_rows, mixed_rows = (
        lax.all_to_all(
            out_grad[0].reshape(group_count, quarter, shard_len),
            "seq",
            split_axis=1,
            concat_axis=2,
            tiled=True,
        ),
        lax.all_to_all(
            mixed.reshape(group_count, quarter, shard_len),
            "seq",
            split_axis=1,
            concat_axis=2,
            tiled=True,
        ),
    )
    filter_grouped = filter_taps.reshape(group_count, quarter, shard_len)
    filter_rows = lax.all_to_all(filter_grouped, "seq", split_axis=1, concat_axis=2, tiled=True)
    grad_real, grad_imag = spectrum(
        grad_rows.reshape(held_channels, length).astype(jnp.float32), tables, columns, coarse
    )
    mix_real, mix_imag = spectrum(
        mixed_rows.reshape(held_channels, length).astype(jnp.float32), tables, columns, coarse
    )
    tap_real, tap_imag = spectrum(
        filter_rows.reshape(held_channels, length), tables, columns, precise
    )
    carry_real = tap_real * grad_real + tap_imag * grad_imag
    carry_imag = tap_real * grad_imag - tap_imag * grad_real
    lag_real = grad_real * mix_real + grad_imag * mix_imag
    lag_imag = grad_imag * mix_real - grad_real * mix_imag
    carried, lagged = to_signal(carry_real - lag_imag, carry_imag + lag_real, tables, length)
    carried = carried.astype(jnp.bfloat16).reshape(group_count, per_block, length)
    returned = lax.all_to_all(carried, "seq", split_axis=2, concat_axis=1, tiled=True)
    carried_home = returned.reshape(channels, shard_len).astype(jnp.float32)
    lagged = lagged.reshape(group_count, per_block, length)
    summed = lax.psum_scatter(lagged, "dp", scatter_dimension=0, tiled=True)
    grad_filter = lax.all_to_all(summed, "seq", split_axis=2, concat_axis=1, tiled=True).reshape(
        quarter, shard_len
    )
    grad_gate = (carried_home * values_wide).astype(jnp.bfloat16)[None]
    grad_values = (carried_home * gate_wide).astype(jnp.bfloat16)[None]
    return (grad_gate, grad_values, grad_filter)


def pack_body(
    groups, own_ref, gate_ref, values_ref, grad_ref, taps_ref, out_ref, gate, values, taps, sems
):
    part = gate.shape[2]
    loads = {}
    loads["taps", 0] = pltpu.make_async_copy(
        taps_ref.at[own_ref[0]], taps, sems.at[3 * groups]
    )
    for q in range(groups):
        loads["gate", q] = pltpu.make_async_copy(gate_ref.at[q], gate.at[q], sems.at[2 * q])
        loads["values", q] = pltpu.make_async_copy(
            values_ref.at[q], values.at[q], sems.at[2 * q + 1]
        )
    for q in range(groups):
        loads["grad", q] = pltpu.make_async_copy(
            grad_ref.at[q], out_ref.at[:, pl.ds(q * part, part), :], sems.at[2 * groups + q]
        )
    for copy in loads.values():
        copy.start()
    loads["taps", 0].wait()
    high = taps[...].astype(jnp.bfloat16)
    out_ref[:, 2 * groups * part : (2 * groups + 1) * part, :] = high
    out_ref[:, (2 * groups + 1) * part :, :] = (taps[...] - high.astype(jnp.float32)).astype(
        jnp.bfloat16
    )
    for q in range(groups):
        loads["gate", q].wait()
        loads["values", q].wait()
        product = gate[q].astype(jnp.float32) * values[q].astype(jnp.float32)
        out_ref[:, (groups + q) * part : (groups + q + 1) * part, :] = product.astype(jnp.bfloat16)
    for q in range(groups):
        loads["grad", q].wait()


def correlate_body(seqs, blocks, unroll, in_ref, out_ref, gs, ms, fs, cs, rs, pads, hs0, ts0, tn0, hs1, ts1, tn1):
    peers = seqs * blocks
    part = in_ref.shape[1] // (2 * seqs + 2)
    held = seqs * part
    steps = LANES // REACH
    near = lax.broadcasted_iota(jnp.int32, (REACH, LANES), 0)
    lane = lax.broadcasted_iota(jnp.int32, (REACH, LANES), 1)
    flip = jnp.where(lane % REACH + near == REACH - 1, 1.0, 0.0).astype(jnp.bfloat16)
    ours = lax.broadcasted_iota(jnp.int32, (peers, LANES), 1) // REACH
    inside = lane + REACH - 1 - near < LANES
    ahead = lane >= near
    deep = lax.broadcasted_iota(jnp.int32, (blocks, LANES), 0)
    thin = lax.broadcasted_iota(jnp.int32, (blocks, LANES), 1)
    across = (((1,), (1,)), ((), ()))
    span = blocks * held
    for b in range(seqs):
        mine = slice(b * blocks, (b + 1) * blocks)
        gs[pl.ds(b * span, span), :] = (
            in_ref[mine, :held, :].astype(jnp.float32).reshape(span, LANES)
        )
        ms[pl.ds(b * span, span), :] = (
            in_ref[mine, held : 2 * held, :].astype(jnp.float32).reshape(span, LANES)
        )
        for s in range(blocks):
            high = in_ref[b * blocks + s, 2 * held : 2 * held + part, :].astype(jnp.float32)
            low = in_ref[b * blocks + s, 2 * held + part :, :].astype(jnp.float32)
            fs[pl.ds(s * held + b * part, part), :] = high + low
    pads[...] = jnp.zeros_like(pads)

    def at(u, q, b):
        return ((u * steps + q) * seqs + b) * 2 * blocks

    def turn_over(group, tn):
        for u in range(unroll):
            c = group * unroll + u
            mixed = ms[pl.ds(c, peers, stride=held), :]
            mixed = jnp.concatenate(
                [jnp.where(ours == q, mixed, 0.0).astype(jnp.bfloat16) for q in range(steps)], axis=0
            )
            tn[u] = lax.dot_general(
                flip, mixed, across, preferred_element_type=jnp.float32
            ).astype(jnp.bfloat16)

    def build(group, hs, ts):
        for u in range(unroll):
            c = group * unroll + u
            for b in range(seqs):
                pads[pl.ds(at(u, 0, b), blocks), :] = gs[pl.ds(b * span + c, blocks, stride=held), :]
        for u in range(unroll):
            for q in range(1, steps):
                for b in range(seqs):
                    here = pads[pl.ds(at(u, 0, b), blocks), :]
                    then = pads[pl.ds(at(u, 0, b) + 1, blocks), :]
                    pads[pl.ds(at(u, q, b), blocks), :] = pltpu.roll(
                        jnp.where(thin >= q * REACH, here, then), LANES - q * REACH, 1
                    )
        for u in range(unroll):
            c = group * unroll + u
            taps = fs[pl.ds(c, blocks, stride=held), :]
            before = jnp.zeros((REACH, LANES), jnp.float32)
            for k in range(blocks):
                turn = pltpu.roll(
                    jnp.broadcast_to(taps[k : k + 1, :], (REACH, LANES)),
                    0,
                    1,
                    stride=1,
                    stride_axis=0,
                )
                block = jnp.where(ahead, turn, before)
                before = turn
                top = block.astype(jnp.bfloat16)
                ts[u, k, :REACH, :] = top
                ts[u, k, REACH:, :] = (block - top.astype(jnp.float32)).astype(jnp.bfloat16)
        for u in range(unroll):
            for q in range(steps):
                for k in range(blocks):
                    hs[u, k, q * peers : (q + 1) * peers, :] = jnp.concatenate(
                        [pads[pl.ds(at(u, q, b) + k, blocks), :] for b in range(seqs)], axis=0
                    ).astype(jnp.bfloat16)

    def joined(ref, u):
        return jnp.concatenate([ref[u, k] for k in range(blocks)], axis=1)

    def merged(parts):
        gap = 1
        while len(parts) > 1:
            keep = deep & gap == 0
            parts = [
                jnp.where(keep, x, y) + pltpu.roll(jnp.where(keep, y, x), gap, 0)
                for x, y in zip(parts[0::2], parts[1::2])
            ]
            gap *= 2
        return parts[0]

    def multiply(group, hs, ts, tn):
        for u in range(unroll):
            c = group * unroll + u
            gram = jnp.dot(tn[u], joined(hs, u), preferred_element_type=jnp.float32)
            later = jnp.zeros((REACH, LANES), jnp.float32)
            sums = []
            for k in reversed(range(blocks)):
                turn = pltpu.roll(
                    gram[:, k * LANES : (k + 1) * LANES],
                    LANES + 1 - REACH,
                    1,
                    stride=1,
                    stride_axis=0,
                )
                picked = jnp.where(inside, turn, later)
                sums.append(sum(picked[i : i + blocks] for i in range(0, REACH, blocks)))
                later = turn
            rs[pl.ds(c, blocks, stride=held), :] = merged(sums[::-1])
        for u in range(unroll):
            c = group * unroll + u
            short = lax.dot_general(
                joined(hs, u), joined(ts, u), across, preferred_element_type=jnp.float32
            )
            short = jnp.concatenate(
                [short, jnp.zeros((steps * peers, LANES - 2 * REACH), jnp.float32)], axis=1
            )
            carried = None
            for q in range(steps):
                mine = short[q * peers : (q + 1) * peers]
                both = pltpu.roll(mine, q * REACH, 1) if q else mine
                back = (q - 1) % steps
                both = both + (pltpu.roll(mine, back * REACH, 1) if back else mine)
                carried = both if carried is None else jnp.where(ours == q, both, carried)
            cs[pl.ds(c, peers, stride=held), :] = carried

    total = held // unroll
    turn_over(0, tn0)
    build(0, hs0, ts0)

    def twice(i, carry):
        turn_over(2 * i + 1, tn1)
        multiply(2 * i, hs0, ts0, tn0)
        build(2 * i + 1, hs1, ts1)
        after = jnp.minimum(2 * i + 2, total - 1)
        turn_over(after, tn0)
        multiply(2 * i + 1, hs1, ts1, tn1)
        build(after, hs0, ts0)
        return carry

    lax.fori_loop(0, total // 2, twice, 0)
    out_ref[:, :held, :] = cs[...].reshape(peers, held, LANES).astype(jnp.bfloat16)
    for q in range(seqs):
        for s in range(blocks):
            out_ref[q * blocks + s, held:, :] = rs[pl.ds(s * held + q * part, part), :].astype(
                jnp.bfloat16
            )


def unpack_body(
    groups, home, gate, values, gate_out, values_out, filter_out, gate_made, values_made, sums, sems
):
    part = gate.shape[2]
    sums[...] = home[:, groups * part :, :].astype(jnp.float32)
    sends = [pltpu.make_async_copy(sums, filter_out, sems.at[2 * groups])]
    sends[-1].start()
    for q in range(groups):
        carried = home[:, q * part : (q + 1) * part, :].astype(jnp.float32)
        gate_made[q] = (carried * values[q].astype(jnp.float32)).astype(jnp.bfloat16)
        values_made[q] = (carried * gate[q].astype(jnp.float32)).astype(jnp.bfloat16)
        for i, (made, out) in enumerate(((gate_made, gate_out), (values_made, values_out))):
            sends.append(pltpu.make_async_copy(made.at[q], out.at[q], sems.at[2 * q + i]))
            sends[-1].start()
    for copy in sends:
        copy.wait()


def correlate(arrived, seqs):
    peers, rows, _ = arrived.shape
    blocks = peers // seqs
    part = rows // (2 * seqs + 2)
    held = seqs * part
    whole = pl.BlockSpec(memory_space=pltpu.VMEM)
    return pl.pallas_call(
        functools.partial(correlate_body, seqs, blocks, UNROLL),
        out_shape=jax.ShapeDtypeStruct((peers, held + part, LANES), jnp.bfloat16),
        in_specs=[whole],
        out_specs=whole,
        scratch_shapes=[
            pltpu.VMEM((peers * held, LANES), jnp.float32),
            pltpu.VMEM((peers * held, LANES), jnp.float32),
            pltpu.VMEM((blocks * held, LANES), jnp.float32),
            pltpu.VMEM((peers * held, LANES), jnp.float32),
            pltpu.VMEM((blocks * held, LANES), jnp.float32),
            pltpu.VMEM((UNROLL * (LANES // REACH) * 2 * peers, LANES), jnp.float32),
            *[
                pltpu.VMEM((UNROLL, blocks, LANES // REACH * peers, LANES), jnp.bfloat16),
                pltpu.VMEM((UNROLL, blocks, 2 * REACH, LANES), jnp.bfloat16),
                pltpu.VMEM((UNROLL, REACH, LANES // REACH * peers), jnp.bfloat16),
            ]
            * 2,
        ],
        cost_estimate=pl.CostEstimate(
            flops=6 * held * LANES * blocks * LANES * peers, bytes_accessed=4 * arrived.size, transcendentals=0
        ),
    )(arrived)


def exchange(array):
    return lax.all_to_all(array, ("dp", "seq"), split_axis=0, concat_axis=0, tiled=True)


def direct_shards(gate_in, values_in, out_grad, filter_taps):
    groups = lax.axis_size("dp")
    peers = groups * lax.axis_size("seq")
    channels = gate_in.shape[1]
    part = channels // (groups * peers)
    shape = (groups, peers, part, LANES)
    gate, values, grad = (array.reshape(shape) for array in (gate_in, values_in, out_grad))
    taps = filter_taps.reshape(shape)
    own = lax.axis_index("dp").astype(jnp.int32).reshape(1)
    far = pl.BlockSpec(memory_space=pl.ANY)
    half = pltpu.VMEM(shape, jnp.bfloat16)
    packed = pl.pallas_call(
        functools.partial(pack_body, groups),
        out_shape=jax.ShapeDtypeStruct((peers, (2 * groups + 2) * part, LANES), jnp.bfloat16),
        in_specs=[pl.BlockSpec(memory_space=pltpu.SMEM), far, far, far, far],
        out_specs=pl.BlockSpec(memory_space=pltpu.VMEM),
        scratch_shapes=[
            half,
            half,
            pltpu.VMEM(shape[1:], jnp.float32),
            pltpu.SemaphoreType.DMA((3 * groups + 1,)),
        ],
    )(own, gate, values, grad, taps)
    near = functools.partial(pltpu.with_memory_space_constraint, memory_space=pltpu.VMEM)
    arrived = near(exchange(packed))
    made = correlate(arrived, groups)
    home = near(exchange(made))
    wide = jax.ShapeDtypeStruct(shape, jnp.bfloat16)
    local = pl.BlockSpec(memory_space=pltpu.VMEM)
    grad_gate, grad_values, grad_filter = pl.pallas_call(
        functools.partial(unpack_body, groups),
        out_shape=(wide, wide, jax.ShapeDtypeStruct(shape[1:], jnp.float32)),
        in_specs=[local, local, local],
        out_specs=(far, far, far),
        scratch_shapes=[
            half,
            half,
            pltpu.VMEM(shape[1:], jnp.float32),
            pltpu.SemaphoreType.DMA((2 * groups + 1,)),
        ],
    )(home, near(gate), near(values))
    return (
        grad_gate.reshape(gate_in.shape),
        grad_values.reshape(gate_in.shape),
        grad_filter.reshape(channels // groups, LANES),
    )


def shards(gate_in, values_in, out_grad, filter_taps):
    groups = lax.axis_size("dp")
    peers = groups * lax.axis_size("seq")
    channels, shard_len = gate_in.shape[1:]
    part = channels // (groups * peers)
    fits = 24 * channels * LANES * groups <= ROOM
    if shard_len == LANES and channels == part * groups * peers and part % SUBLANES == 0 and fits:
        return direct_shards(gate_in, values_in, out_grad, filter_taps)
    return spectral_shards(gate_in, values_in, out_grad, filter_taps)


def solution(mesh):
    return jax.shard_map(
        shards,
        mesh=mesh,
        in_specs=(P("dp", None, "seq"), P("dp", None, "seq"), P("dp", None, "seq"), P(None, "seq")),
        out_specs=(P("dp", None, "seq"), P("dp", None, "seq"), P("dp", "seq")),
        check_vma=False,
    )
```

```python
import functools
import math

import jax
import jax.numpy as jnp
from jax import lax
from jax.experimental import pallas as pl
from jax.experimental.pallas import tpu as pltpu
from jax.sharding import PartitionSpec as P

LANES = 128
SUBLANES = 16
REACH = 32
UNROLL = 8
EARLY = 96
ROOM = 40 * 2**20

precise = lax.Precision.HIGHEST
coarse = lax.Precision.HIGH


def spin_tables(count_in, count_out, period):
    rows = lax.broadcasted_iota(jnp.int32, (count_in, count_out), 0)
    cols = lax.broadcasted_iota(jnp.int32, (count_in, count_out), 1)
    phase = (rows * cols % period).astype(jnp.float32) * (2.0 * math.pi / period)
    return (jnp.cos(phase), jnp.sin(phase))


def make_tables(length, columns):
    rows_in = length // columns
    rows_out = 2 * rows_in
    first_cos, first_sin = spin_tables(rows_in, rows_out, rows_out)
    turn = spin_tables(rows_out, columns, 2 * length)
    last_cos, last_sin = spin_tables(columns, columns, columns)
    first_fwd = jnp.concatenate([first_cos, -first_sin], axis=1)
    last_fwd = jnp.concatenate(
        [
            jnp.concatenate([last_cos, -last_sin], axis=1),
            jnp.concatenate([last_sin, last_cos], axis=1),
        ],
        axis=0,
    )
    last_inv = jnp.concatenate(
        [
            jnp.concatenate([last_cos.T, last_sin.T], axis=1),
            jnp.concatenate([-last_sin.T, last_cos.T], axis=1),
        ],
        axis=0,
    )
    first_inv = jnp.concatenate(
        [
            jnp.concatenate([first_cos.T, first_sin.T], axis=1),
            jnp.concatenate([-first_sin.T, first_cos.T], axis=1),
        ],
        axis=0,
    )
    return (first_fwd, turn, last_fwd, last_inv, first_inv)


def spectrum(signal, tables, columns, first_precision):
    first_fwd, (turn_cos, turn_sin), last_fwd, last_inv, first_inv = tables
    held, length = signal.shape
    half = turn_cos.shape[0]
    grid = signal.reshape(held, length // columns, columns)
    part = jnp.einsum("cmn,mk->ckn", grid, first_fwd, precision=first_precision)
    part_real = part[:, :half]
    part_imag = part[:, half:]
    turned = jnp.concatenate(
        [part_real * turn_cos + part_imag * turn_sin, part_imag * turn_cos - part_real * turn_sin],
        axis=2,
    )
    out = jnp.einsum("ckn,nj->ckj", turned, last_fwd, precision=first_precision)
    return (out[:, :, :columns], out[:, :, columns:])


def to_signal(spec_real, spec_imag, tables, length):
    first_fwd, (turn_cos, turn_sin), last_fwd, last_inv, first_inv = tables
    held = spec_real.shape[0]
    columns = spec_real.shape[2]
    rows_in = length // columns
    stacked = jnp.concatenate([spec_real, spec_imag], axis=2)
    back = jnp.einsum("ckj,jn->ckn", stacked, last_inv, precision=coarse)
    back_real = back[:, :, :columns]
    back_imag = back[:, :, columns:]
    turned = jnp.concatenate(
        [back_real * turn_cos - back_imag * turn_sin, back_imag * turn_cos + back_real * turn_sin],
        axis=1,
    )
    factor = 1.0 / (2 * length)
    both = jnp.einsum("ckn,km->cmn", turned, first_inv, precision=coarse) * factor
    real_part = both[:, :rows_in]
    imag_part = both[:, rows_in:]
    return (real_part.reshape(held, length), imag_part.reshape(held, length))


def spectral_shards(gate_in, values_in, out_grad, filter_taps):
    seq_count = lax.axis_size("seq")
    group_count = lax.axis_size("dp")
    channels = gate_in.shape[1]
    shard_len = gate_in.shape[2]
    length = shard_len * seq_count
    quarter = channels // group_count
    per_block = quarter // seq_count
    held_channels = group_count * per_block
    columns = 128 if length % 128 == 0 and length >= 8192 else 32
    tables = make_tables(length, columns)
    gate_wide = gate_in[0].astype(jnp.float32)
    values_wide = values_in[0].astype(jnp.float32)
    mixed = (gate_wide * values_wide).astype(jnp.bfloat16)
    grad_rows, mixed_rows = (
        lax.all_to_all(
            out_grad[0].reshape(group_count, quarter, shard_len),
            "seq",
            split_axis=1,
            concat_axis=2,
            tiled=True,
        ),
        lax.all_to_all(
            mixed.reshape(group_count, quarter, shard_len),
            "seq",
            split_axis=1,
            concat_axis=2,
            tiled=True,
        ),
    )
    filter_grouped = filter_taps.reshape(group_count, quarter, shard_len)
    filter_rows = lax.all_to_all(filter_grouped, "seq", split_axis=1, concat_axis=2, tiled=True)
    grad_real, grad_imag = spectrum(
        grad_rows.reshape(held_channels, length).astype(jnp.float32), tables, columns, coarse
    )
    mix_real, mix_imag = spectrum(
        mixed_rows.reshape(held_channels, length).astype(jnp.float32), tables, columns, coarse
    )
    tap_real, tap_imag = spectrum(
        filter_rows.reshape(held_channels, length), tables, columns, precise
    )
    carry_real = tap_real * grad_real + tap_imag * grad_imag
    carry_imag = tap_real * grad_imag - tap_imag * grad_real
    lag_real = grad_real * mix_real + grad_imag * mix_imag
    lag_imag = grad_imag * mix_real - grad_real * mix_imag
    carried, lagged = to_signal(carry_real - lag_imag, carry_imag + lag_real, tables, length)
    carried = carried.astype(jnp.bfloat16).reshape(group_count, per_block, length)
    returned = lax.all_to_all(carried, "seq", split_axis=2, concat_axis=1, tiled=True)
    carried_home = returned.reshape(channels, shard_len).astype(jnp.float32)
    lagged = lagged.reshape(group_count, per_block, length)
    summed = lax.psum_scatter(lagged, "dp", scatter_dimension=0, tiled=True)
    grad_filter = lax.all_to_all(summed, "seq", split_axis=2, concat_axis=1, tiled=True).reshape(
        quarter, shard_len
    )
    grad_gate = (carried_home * values_wide).astype(jnp.bfloat16)[None]
    grad_values = (carried_home * gate_wide).astype(jnp.bfloat16)[None]
    return (grad_gate, grad_values, grad_filter)


def pack_body(
    first, count, own_ref, gate_ref, values_ref, grad_ref, taps_ref, out_ref, gate, values, taps, sems
):
    part = gate.shape[2]
    loads = {}
    if not first:
        loads["taps", 0] = pltpu.make_async_copy(
            taps_ref.at[own_ref[0]], taps, sems.at[3 * count]
        )
    for i in range(count):
        q = first + i
        loads["gate", i] = pltpu.make_async_copy(gate_ref.at[q], gate.at[i], sems.at[2 * i])
        loads["values", i] = pltpu.make_async_copy(
            values_ref.at[q], values.at[i], sems.at[2 * i + 1]
        )
    for i in range(count):
        loads["grad", i] = pltpu.make_async_copy(
            grad_ref.at[first + i],
            out_ref.at[:, pl.ds(i * part, part), :],
            sems.at[2 * count + i],
        )
    for copy in loads.values():
        copy.start()
    if not first:
        loads["taps", 0].wait()
        high = taps[...].astype(jnp.bfloat16)
        out_ref[:, 2 * count * part : (2 * count + 1) * part, :] = high
        out_ref[:, (2 * count + 1) * part :, :] = (taps[...] - high.astype(jnp.float32)).astype(
            jnp.bfloat16
        )
    for i in range(count):
        loads["gate", i].wait()
        loads["values", i].wait()
        product = gate[i].astype(jnp.float32) * values[i].astype(jnp.float32)
        out_ref[:, (count + i) * part : (count + i + 1) * part, :] = product.astype(jnp.bfloat16)
    for i in range(count):
        loads["grad", i].wait()


def correlate_body(seqs, blocks, unroll, part, first, count, *refs):
    peers = seqs * blocks
    held = count * part
    if first:
        in_ref, taps_ref, early_ref, early_sums_ref, out_ref, *refs = refs
    else:
        in_ref, out_ref, sums_ref, *refs = refs
        taps_ref = in_ref
    gs, ms, fs, cs, rs, pads, hs0, ts0, tn0, hs1, ts1, tn1, sems = refs
    moves = []
    if first:
        moves = [
            pltpu.make_async_copy(
                early_ref, out_ref.at[:, pl.ds(0, first * part), :], sems.at[0]
            ),
            pltpu.make_async_copy(
                early_sums_ref,
                out_ref.at[pl.ds(0, first * blocks), pl.ds(seqs * part, part), :],
                sems.at[1],
            ),
        ]
    for move in moves:
        move.start()
    steps = LANES // REACH
    near = lax.broadcasted_iota(jnp.int32, (REACH, LANES), 0)
    lane = lax.broadcasted_iota(jnp.int32, (REACH, LANES), 1)
    flip = jnp.where(lane % REACH + near == REACH - 1, 1.0, 0.0).astype(jnp.bfloat16)
    ours = lax.broadcasted_iota(jnp.int32, (peers, LANES), 1) // REACH
    inside = lane + REACH - 1 - near < LANES
    ahead = lane >= near
    deep = lax.broadcasted_iota(jnp.int32, (blocks, LANES), 0)
    thin = lax.broadcasted_iota(jnp.int32, (blocks, LANES), 1)
    across = (((1,), (1,)), ((), ()))
    span = blocks * held
    for b in range(seqs):
        mine = slice(b * blocks, (b + 1) * blocks)
        gs[pl.ds(b * span, span), :] = (
            in_ref[mine, :held, :].astype(jnp.float32).reshape(span, LANES)
        )
        ms[pl.ds(b * span, span), :] = (
            in_ref[mine, held : 2 * held, :].astype(jnp.float32).reshape(span, LANES)
        )
    base = taps_ref.shape[1] - 2 * part
    for i in range(count):
        for s in range(blocks):
            p = (first + i) * blocks + s
            high = taps_ref[p, base : base + part, :].astype(jnp.float32)
            low = taps_ref[p, base + part :, :].astype(jnp.float32)
            fs[pl.ds(s * held + i * part, part), :] = high + low
    pads[...] = jnp.zeros_like(pads)

    def at(u, q, b):
        return ((u * steps + q) * seqs + b) * 2 * blocks

    def turn_over(group, tn):
        for u in range(unroll):
            c = group * unroll + u
            mixed = ms[pl.ds(c, peers, stride=held), :]
            mixed = jnp.concatenate(
                [jnp.where(ours == q, mixed, 0.0).astype(jnp.bfloat16) for q in range(steps)], axis=0
            )
            tn[u] = lax.dot_general(
                flip, mixed, across, preferred_element_type=jnp.float32
            ).astype(jnp.bfloat16)

    def build(group, hs, ts):
        for u in range(unroll):
            c = group * unroll + u
            for b in range(seqs):
                pads[pl.ds(at(u, 0, b), blocks), :] = gs[pl.ds(b * span + c, blocks, stride=held), :]
        for u in range(unroll):
            for q in range(1, steps):
                for b in range(seqs):
                    here = pads[pl.ds(at(u, 0, b), blocks), :]
                    then = pads[pl.ds(at(u, 0, b) + 1, blocks), :]
                    pads[pl.ds(at(u, q, b), blocks), :] = pltpu.roll(
                        jnp.where(thin >= q * REACH, here, then), LANES - q * REACH, 1
                    )
        for u in range(unroll):
            c = group * unroll + u
            taps = fs[pl.ds(c, blocks, stride=held), :]
            before = jnp.zeros((REACH, LANES), jnp.float32)
            for k in range(blocks):
                turn = pltpu.roll(
                    jnp.broadcast_to(taps[k : k + 1, :], (REACH, LANES)),
                    0,
                    1,
                    stride=1,
                    stride_axis=0,
                )
                block = jnp.where(ahead, turn, before)
                before = turn
                top = block.astype(jnp.bfloat16)
                ts[u, k, :REACH, :] = top
                ts[u, k, REACH:, :] = (block - top.astype(jnp.float32)).astype(jnp.bfloat16)
        for u in range(unroll):
            for q in range(steps):
                for k in range(blocks):
                    hs[u, k, q * peers : (q + 1) * peers, :] = jnp.concatenate(
                        [pads[pl.ds(at(u, q, b) + k, blocks), :] for b in range(seqs)], axis=0
                    ).astype(jnp.bfloat16)

    def joined(ref, u):
        return jnp.concatenate([ref[u, k] for k in range(blocks)], axis=1)

    def merged(parts):
        gap = 1
        while len(parts) > 1:
            keep = deep & gap == 0
            parts = [
                jnp.where(keep, x, y) + pltpu.roll(jnp.where(keep, y, x), gap, 0)
                for x, y in zip(parts[0::2], parts[1::2])
            ]
            gap *= 2
        return parts[0]

    def multiply(group, hs, ts, tn):
        for u in range(unroll):
            c = group * unroll + u
            gram = jnp.dot(tn[u], joined(hs, u), preferred_element_type=jnp.float32)
            later = jnp.zeros((REACH, LANES), jnp.float32)
            sums = []
            for k in reversed(range(blocks)):
                turn = pltpu.roll(
                    gram[:, k * LANES : (k + 1) * LANES],
                    LANES + 1 - REACH,
                    1,
                    stride=1,
                    stride_axis=0,
                )
                picked = jnp.where(inside, turn, later)
                sums.append(sum(picked[i : i + blocks] for i in range(0, REACH, blocks)))
                later = turn
            rs[pl.ds(c, blocks, stride=held), :] = merged(sums[::-1])
        for u in range(unroll):
            c = group * unroll + u
            short = lax.dot_general(
                joined(hs, u), joined(ts, u), across, preferred_element_type=jnp.float32
            )
            short = jnp.concatenate(
                [short, jnp.zeros((steps * peers, LANES - 2 * REACH), jnp.float32)], axis=1
            )
            carried = None
            for q in range(steps):
                mine = short[q * peers : (q + 1) * peers]
                both = pltpu.roll(mine, q * REACH, 1) if q else mine
                back = (q - 1) % steps
                both = both + (pltpu.roll(mine, back * REACH, 1) if back else mine)
                carried = both if carried is None else jnp.where(ours == q, both, carried)
            cs[pl.ds(c, peers, stride=held), :] = carried

    total = held // unroll
    turn_over(0, tn0)
    build(0, hs0, ts0)

    def twice(i, carry):
        turn_over(2 * i + 1, tn1)
        multiply(2 * i, hs0, ts0, tn0)
        build(2 * i + 1, hs1, ts1)
        after = jnp.minimum(2 * i + 2, total - 1)
        turn_over(after, tn0)
        multiply(2 * i + 1, hs1, ts1, tn1)
        build(after, hs0, ts0)
        return carry

    lax.fori_loop(0, total // 2, twice, 0)
    made = cs[...].reshape(peers, held, LANES).astype(jnp.bfloat16)
    ahead_rows = first * part
    out_ref[:, ahead_rows : ahead_rows + held, :] = made
    for i in range(count):
        for s in range(blocks):
            block = rs[pl.ds(s * held + i * part, part), :].astype(jnp.bfloat16)
            if first:
                out_ref[(first + i) * blocks + s, seqs * part :, :] = block
            else:
                sums_ref[i * blocks + s] = block
    for move in moves:
        move.wait()


def unpack_body(
    groups, home, gate, values, gate_out, values_out, filter_out, gate_made, values_made, sums, sems
):
    part = gate.shape[2]
    sums[...] = home[:, groups * part :, :].astype(jnp.float32)
    sends = [pltpu.make_async_copy(sums, filter_out, sems.at[2 * groups])]
    sends[-1].start()
    for q in range(groups):
        carried = home[:, q * part : (q + 1) * part, :].astype(jnp.float32)
        gate_made[q] = (carried * values[q].astype(jnp.float32)).astype(jnp.bfloat16)
        values_made[q] = (carried * gate[q].astype(jnp.float32)).astype(jnp.bfloat16)
        for i, (made, out) in enumerate(((gate_made, gate_out), (values_made, values_out))):
            sends.append(pltpu.make_async_copy(made.at[q], out.at[q], sems.at[2 * q + i]))
            sends[-1].start()
    for copy in sends:
        copy.wait()


def correlate(seqs, part, first, count, *arrays):
    peers = arrays[0].shape[0]
    blocks = peers // seqs
    held = count * part
    whole = pl.BlockSpec(memory_space=pltpu.VMEM)
    if first:
        out_shape = (jax.ShapeDtypeStruct((peers, (seqs + 1) * part, LANES), jnp.bfloat16),)
    else:
        out_shape = (
            jax.ShapeDtypeStruct((peers, held, LANES), jnp.bfloat16),
            jax.ShapeDtypeStruct((count * blocks, part, LANES), jnp.bfloat16),
        )
    return pl.pallas_call(
        functools.partial(correlate_body, seqs, blocks, UNROLL, part, first, count),
        out_shape=out_shape,
        in_specs=[whole] * min(len(arrays), 2) + [pl.BlockSpec(memory_space=pl.ANY)] * (len(arrays) - 2),
        out_specs=(whole,) * len(out_shape),
        scratch_shapes=[
            pltpu.VMEM((peers * held, LANES), jnp.float32),
            pltpu.VMEM((peers * held, LANES), jnp.float32),
            pltpu.VMEM((blocks * held, LANES), jnp.float32),
            pltpu.VMEM((peers * held, LANES), jnp.float32),
            pltpu.VMEM((blocks * held, LANES), jnp.float32),
            pltpu.VMEM((UNROLL * (LANES // REACH) * 2 * peers, LANES), jnp.float32),
            *[
                pltpu.VMEM((UNROLL, blocks, LANES // REACH * peers, LANES), jnp.bfloat16),
                pltpu.VMEM((UNROLL, blocks, 2 * REACH, LANES), jnp.bfloat16),
                pltpu.VMEM((UNROLL, REACH, LANES // REACH * peers), jnp.bfloat16),
            ]
            * 2,
            pltpu.SemaphoreType.DMA((2,)),
        ],
        cost_estimate=pl.CostEstimate(
            flops=60 * held * LANES * blocks * LANES * peers,
            bytes_accessed=4 * arrays[0].size,
            transcendentals=0,
        ),
    )(*arrays)


def exchange(array):
    return lax.all_to_all(array, ("dp", "seq"), split_axis=0, concat_axis=0, tiled=True)


def direct_shards(gate_in, values_in, out_grad, filter_taps):
    groups = lax.axis_size("dp")
    peers = groups * lax.axis_size("seq")
    channels = gate_in.shape[1]
    part = channels // (groups * peers)
    shape = (groups, peers, part, LANES)
    gate, values, grad = (array.reshape(shape) for array in (gate_in, values_in, out_grad))
    taps = filter_taps.reshape(shape)
    own = lax.axis_index("dp").astype(jnp.int32).reshape(1)
    far = pl.BlockSpec(memory_space=pl.ANY)
    half = pltpu.VMEM(shape, jnp.bfloat16)
    near = functools.partial(pltpu.with_memory_space_constraint, memory_space=pltpu.VMEM)
    early = groups * EARLY // LANES
    late = groups - early

    def pack(first, count):
        rows = (2 * count + (0 if first else 2)) * part
        kept = pltpu.VMEM((count,) + shape[1:], jnp.bfloat16)
        return pl.pallas_call(
            functools.partial(pack_body, first, count),
            out_shape=jax.ShapeDtypeStruct((peers, rows, LANES), jnp.bfloat16),
            in_specs=[pl.BlockSpec(memory_space=pltpu.SMEM), far, far, far, far],
            out_specs=pl.BlockSpec(memory_space=pltpu.VMEM),
            scratch_shapes=[
                kept,
                kept,
                pltpu.VMEM(shape[1:], jnp.float32),
                pltpu.SemaphoreType.DMA((3 * count + 1,)),
            ],
        )(own, gate, values, grad, taps)

    arrived = near(exchange(pack(0, early)))
    rest = near(exchange(pack(early, late)))
    made, sums = correlate(groups, part, 0, early, arrived)
    (made,) = correlate(groups, part, early, late, rest, arrived, made, sums)
    home = near(exchange(made))
    wide = jax.ShapeDtypeStruct(shape, jnp.bfloat16)
    local = pl.BlockSpec(memory_space=pltpu.VMEM)
    grad_gate, grad_values, grad_filter = pl.pallas_call(
        functools.partial(unpack_body, groups),
        out_shape=(wide, wide, jax.ShapeDtypeStruct(shape[1:], jnp.float32)),
        in_specs=[local, local, local],
        out_specs=(far, far, far),
        scratch_shapes=[
            half,
            half,
            pltpu.VMEM(shape[1:], jnp.float32),
            pltpu.SemaphoreType.DMA((2 * groups + 1,)),
        ],
    )(home, near(gate), near(values))
    return (
        grad_gate.reshape(gate_in.shape),
        grad_values.reshape(gate_in.shape),
        grad_filter.reshape(channels // groups, LANES),
    )


def shards(gate_in, values_in, out_grad, filter_taps):
    groups = lax.axis_size("dp")
    peers = groups * lax.axis_size("seq")
    channels, shard_len = gate_in.shape[1:]
    part = channels // (groups * peers)
    fits = 24 * channels * LANES * groups <= ROOM
    if shard_len == LANES and channels == part * groups * peers and part % SUBLANES == 0 and fits:
        return direct_shards(gate_in, values_in, out_grad, filter_taps)
    return spectral_shards(gate_in, values_in, out_grad, filter_taps)


def solution(mesh):
    return jax.shard_map(
        shards,
        mesh=mesh,
        in_specs=(P("dp", None, "seq"), P("dp", None, "seq"), P("dp", None, "seq"), P(None, "seq")),
        out_specs=(P("dp", None, "seq"), P("dp", None, "seq"), P("dp", "seq")),
        check_vma=False,
    )
```

```python
import functools
import math

import jax
import jax.numpy as jnp
from jax import lax
from jax.experimental import pallas as pl
from jax.experimental.pallas import tpu as pltpu
from jax.sharding import PartitionSpec as P

LANES = 128
SUBLANES = 16
REACH = 32
UNROLL = 8
PIECES = 4
ROOM = 40 * 2**20

precise = lax.Precision.HIGHEST
coarse = lax.Precision.HIGH


def spin_tables(count_in, count_out, period):
    rows = lax.broadcasted_iota(jnp.int32, (count_in, count_out), 0)
    cols = lax.broadcasted_iota(jnp.int32, (count_in, count_out), 1)
    phase = (rows * cols % period).astype(jnp.float32) * (2.0 * math.pi / period)
    return (jnp.cos(phase), jnp.sin(phase))


def make_tables(length, columns):
    rows_in = length // columns
    rows_out = 2 * rows_in
    first_cos, first_sin = spin_tables(rows_in, rows_out, rows_out)
    turn = spin_tables(rows_out, columns, 2 * length)
    last_cos, last_sin = spin_tables(columns, columns, columns)
    first_fwd = jnp.concatenate([first_cos, -first_sin], axis=1)
    last_fwd = jnp.concatenate(
        [
            jnp.concatenate([last_cos, -last_sin], axis=1),
            jnp.concatenate([last_sin, last_cos], axis=1),
        ],
        axis=0,
    )
    last_inv = jnp.concatenate(
        [
            jnp.concatenate([last_cos.T, last_sin.T], axis=1),
            jnp.concatenate([-last_sin.T, last_cos.T], axis=1),
        ],
        axis=0,
    )
    first_inv = jnp.concatenate(
        [
            jnp.concatenate([first_cos.T, first_sin.T], axis=1),
            jnp.concatenate([-first_sin.T, first_cos.T], axis=1),
        ],
        axis=0,
    )
    return (first_fwd, turn, last_fwd, last_inv, first_inv)


def spectrum(signal, tables, columns, first_precision):
    first_fwd, (turn_cos, turn_sin), last_fwd, last_inv, first_inv = tables
    held, length = signal.shape
    half = turn_cos.shape[0]
    grid = signal.reshape(held, length // columns, columns)
    part = jnp.einsum("cmn,mk->ckn", grid, first_fwd, precision=first_precision)
    part_real = part[:, :half]
    part_imag = part[:, half:]
    turned = jnp.concatenate(
        [part_real * turn_cos + part_imag * turn_sin, part_imag * turn_cos - part_real * turn_sin],
        axis=2,
    )
    out = jnp.einsum("ckn,nj->ckj", turned, last_fwd, precision=first_precision)
    return (out[:, :, :columns], out[:, :, columns:])


def to_signal(spec_real, spec_imag, tables, length):
    first_fwd, (turn_cos, turn_sin), last_fwd, last_inv, first_inv = tables
    held = spec_real.shape[0]
    columns = spec_real.shape[2]
    rows_in = length // columns
    stacked = jnp.concatenate([spec_real, spec_imag], axis=2)
    back = jnp.einsum("ckj,jn->ckn", stacked, last_inv, precision=coarse)
    back_real = back[:, :, :columns]
    back_imag = back[:, :, columns:]
    turned = jnp.concatenate(
        [back_real * turn_cos - back_imag * turn_sin, back_imag * turn_cos + back_real * turn_sin],
        axis=1,
    )
    factor = 1.0 / (2 * length)
    both = jnp.einsum("ckn,km->cmn", turned, first_inv, precision=coarse) * factor
    real_part = both[:, :rows_in]
    imag_part = both[:, rows_in:]
    return (real_part.reshape(held, length), imag_part.reshape(held, length))


def spectral_shards(gate_in, values_in, out_grad, filter_taps):
    seq_count = lax.axis_size("seq")
    group_count = lax.axis_size("dp")
    channels = gate_in.shape[1]
    shard_len = gate_in.shape[2]
    length = shard_len * seq_count
    quarter = channels // group_count
    per_block = quarter // seq_count
    held_channels = group_count * per_block
    columns = 128 if length % 128 == 0 and length >= 8192 else 32
    tables = make_tables(length, columns)
    gate_wide = gate_in[0].astype(jnp.float32)
    values_wide = values_in[0].astype(jnp.float32)
    mixed = (gate_wide * values_wide).astype(jnp.bfloat16)
    grad_rows, mixed_rows = (
        lax.all_to_all(
            out_grad[0].reshape(group_count, quarter, shard_len),
            "seq",
            split_axis=1,
            concat_axis=2,
            tiled=True,
        ),
        lax.all_to_all(
            mixed.reshape(group_count, quarter, shard_len),
            "seq",
            split_axis=1,
            concat_axis=2,
            tiled=True,
        ),
    )
    filter_grouped = filter_taps.reshape(group_count, quarter, shard_len)
    filter_rows = lax.all_to_all(filter_grouped, "seq", split_axis=1, concat_axis=2, tiled=True)
    grad_real, grad_imag = spectrum(
        grad_rows.reshape(held_channels, length).astype(jnp.float32), tables, columns, coarse
    )
    mix_real, mix_imag = spectrum(
        mixed_rows.reshape(held_channels, length).astype(jnp.float32), tables, columns, coarse
    )
    tap_real, tap_imag = spectrum(
        filter_rows.reshape(held_channels, length), tables, columns, precise
    )
    carry_real = tap_real * grad_real + tap_imag * grad_imag
    carry_imag = tap_real * grad_imag - tap_imag * grad_real
    lag_real = grad_real * mix_real + grad_imag * mix_imag
    lag_imag = grad_imag * mix_real - grad_real * mix_imag
    carried, lagged = to_signal(carry_real - lag_imag, carry_imag + lag_real, tables, length)
    carried = carried.astype(jnp.bfloat16).reshape(group_count, per_block, length)
    returned = lax.all_to_all(carried, "seq", split_axis=2, concat_axis=1, tiled=True)
    carried_home = returned.reshape(channels, shard_len).astype(jnp.float32)
    lagged = lagged.reshape(group_count, per_block, length)
    summed = lax.psum_scatter(lagged, "dp", scatter_dimension=0, tiled=True)
    grad_filter = lax.all_to_all(summed, "seq", split_axis=2, concat_axis=1, tiled=True).reshape(
        quarter, shard_len
    )
    grad_gate = (carried_home * values_wide).astype(jnp.bfloat16)[None]
    grad_values = (carried_home * gate_wide).astype(jnp.bfloat16)[None]
    return (grad_gate, grad_values, grad_filter)


def pack_body(
    groups, pieces, own_ref, gate_ref, values_ref, grad_ref, taps_ref, out_ref,
    gate, values, taps, made, in_sems, out_sems,
):
    peers, part = gate.shape[1:3]
    size = peers // pieces
    loads = []
    for j in range(pieces):
        own = pl.ds(j * size, size)
        pairs = [
            (gate_ref.at[:, own], gate.at[:, own]),
            (values_ref.at[:, own], values.at[:, own]),
            (taps_ref.at[own_ref[0], own], taps.at[own]),
        ]
        pairs += [
            (grad_ref.at[q, own], made.at[own, pl.ds(q * part, part), :]) for q in range(groups)
        ]
        loads.append(
            [
                pltpu.make_async_copy(source, target, in_sems.at[j, i])
                for i, (source, target) in enumerate(pairs)
            ]
        )
    for copies in loads:
        for copy in copies:
            copy.start()
    sends = []
    for j in range(pieces):
        own = slice(j * size, (j + 1) * size)
        for copy in loads[j][:3]:
            copy.wait()
        for q in range(groups):
            product = gate[q, own].astype(jnp.float32) * values[q, own].astype(jnp.float32)
            made[own, (groups + q) * part : (groups + q + 1) * part, :] = product.astype(jnp.bfloat16)
        high = taps[own].astype(jnp.bfloat16)
        made[own, 2 * groups * part : (2 * groups + 1) * part, :] = high
        made[own, (2 * groups + 1) * part :, :] = (taps[own] - high.astype(jnp.float32)).astype(
            jnp.bfloat16
        )
        for copy in loads[j][3:]:
            copy.wait()
        rows = pl.ds(j * size, size)
        sends.append(pltpu.make_async_copy(made.at[rows], out_ref.at[rows], out_sems.at[j]))
        sends[-1].start()
    for copy in sends:
        copy.wait()


def correlate_body(seqs, blocks, unroll, in_ref, out_ref, gs, ms, fs, cs, rs, pads, hs0, ts0, tn0, hs1, ts1, tn1):
    peers = seqs * blocks
    part = in_ref.shape[1] // (2 * seqs + 2)
    held = seqs * part
    steps = LANES // REACH
    near = lax.broadcasted_iota(jnp.int32, (REACH, LANES), 0)
    lane = lax.broadcasted_iota(jnp.int32, (REACH, LANES), 1)
    flip = jnp.where(lane % REACH + near == REACH - 1, 1.0, 0.0).astype(jnp.bfloat16)
    ours = lax.broadcasted_iota(jnp.int32, (peers, LANES), 1) // REACH
    inside = lane + REACH - 1 - near < LANES
    ahead = lane >= near
    deep = lax.broadcasted_iota(jnp.int32, (blocks, LANES), 0)
    thin = lax.broadcasted_iota(jnp.int32, (blocks, LANES), 1)
    across = (((1,), (1,)), ((), ()))
    span = blocks * held
    for b in range(seqs):
        mine = slice(b * blocks, (b + 1) * blocks)
        gs[pl.ds(b * span, span), :] = (
            in_ref[mine, :held, :].astype(jnp.float32).reshape(span, LANES)
        )
        ms[pl.ds(b * span, span), :] = (
            in_ref[mine, held : 2 * held, :].astype(jnp.float32).reshape(span, LANES)
        )
        for s in range(blocks):
            high = in_ref[b * blocks + s, 2 * held : 2 * held + part, :].astype(jnp.float32)
            low = in_ref[b * blocks + s, 2 * held + part :, :].astype(jnp.float32)
            fs[pl.ds(s * held + b * part, part), :] = high + low
    pads[...] = jnp.zeros_like(pads)

    def at(u, q, b):
        return ((u * steps + q) * seqs + b) * 2 * blocks

    def turn_over(group, tn):
        for u in range(unroll):
            c = group * unroll + u
            mixed = ms[pl.ds(c, peers, stride=held), :]
            mixed = jnp.concatenate(
                [jnp.where(ours == q, mixed, 0.0).astype(jnp.bfloat16) for q in range(steps)], axis=0
            )
            tn[u] = lax.dot_general(
                flip, mixed, across, preferred_element_type=jnp.float32
            ).astype(jnp.bfloat16)

    def build(group, hs, ts):
        for u in range(unroll):
            c = group * unroll + u
            for b in range(seqs):
                pads[pl.ds(at(u, 0, b), blocks), :] = gs[pl.ds(b * span + c, blocks, stride=held), :]
        for u in range(unroll):
            for q in range(1, steps):
                for b in range(seqs):
                    here = pads[pl.ds(at(u, 0, b), blocks), :]
                    then = pads[pl.ds(at(u, 0, b) + 1, blocks), :]
                    pads[pl.ds(at(u, q, b), blocks), :] = pltpu.roll(
                        jnp.where(thin >= q * REACH, here, then), LANES - q * REACH, 1
                    )
        for u in range(unroll):
            c = group * unroll + u
            taps = fs[pl.ds(c, blocks, stride=held), :]
            before = jnp.zeros((REACH, LANES), jnp.float32)
            for k in range(blocks):
                turn = pltpu.roll(
                    jnp.broadcast_to(taps[k : k + 1, :], (REACH, LANES)),
                    0,
                    1,
                    stride=1,
                    stride_axis=0,
                )
                block = jnp.where(ahead, turn, before)
                before = turn
                top = block.astype(jnp.bfloat16)
                ts[u, k, :REACH, :] = top
                ts[u, k, REACH:, :] = (block - top.astype(jnp.float32)).astype(jnp.bfloat16)
        for u in range(unroll):
            for q in range(steps):
                for k in range(blocks):
                    hs[u, k, q * peers : (q + 1) * peers, :] = jnp.concatenate(
                        [pads[pl.ds(at(u, q, b) + k, blocks), :] for b in range(seqs)], axis=0
                    ).astype(jnp.bfloat16)

    def joined(ref, u):
        return jnp.concatenate([ref[u, k] for k in range(blocks)], axis=1)

    def merged(parts):
        gap = 1
        while len(parts) > 1:
            keep = deep & gap == 0
            parts = [
                jnp.where(keep, x, y) + pltpu.roll(jnp.where(keep, y, x), gap, 0)
                for x, y in zip(parts[0::2], parts[1::2])
            ]
            gap *= 2
        return parts[0]

    def multiply(group, hs, ts, tn):
        for u in range(unroll):
            c = group * unroll + u
            gram = jnp.dot(tn[u], joined(hs, u), preferred_element_type=jnp.float32)
            later = jnp.zeros((REACH, LANES), jnp.float32)
            sums = []
            for k in reversed(range(blocks)):
                turn = pltpu.roll(
                    gram[:, k * LANES : (k + 1) * LANES],
                    LANES + 1 - REACH,
                    1,
                    stride=1,
                    stride_axis=0,
                )
                picked = jnp.where(inside, turn, later)
                sums.append(sum(picked[i : i + blocks] for i in range(0, REACH, blocks)))
                later = turn
            rs[pl.ds(c, blocks, stride=held), :] = merged(sums[::-1])
        for u in range(unroll):
            c = group * unroll + u
            short = lax.dot_general(
                joined(hs, u), joined(ts, u), across, preferred_element_type=jnp.float32
            )
            short = jnp.concatenate(
                [short, jnp.zeros((steps * peers, LANES - 2 * REACH), jnp.float32)], axis=1
            )
            carried = None
            for q in range(steps):
                mine = short[q * peers : (q + 1) * peers]
                both = pltpu.roll(mine, q * REACH, 1) if q else mine
                back = (q - 1) % steps
                both = both + (pltpu.roll(mine, back * REACH, 1) if back else mine)
                carried = both if carried is None else jnp.where(ours == q, both, carried)
            cs[pl.ds(c, peers, stride=held), :] = carried

    total = held // unroll
    turn_over(0, tn0)
    build(0, hs0, ts0)

    def twice(i, carry):
        turn_over(2 * i + 1, tn1)
        multiply(2 * i, hs0, ts0, tn0)
        build(2 * i + 1, hs1, ts1)
        after = jnp.minimum(2 * i + 2, total - 1)
        turn_over(after, tn0)
        multiply(2 * i + 1, hs1, ts1, tn1)
        build(after, hs0, ts0)
        return carry

    lax.fori_loop(0, total // 2, twice, 0)
    out_ref[:, :held, :] = cs[...].reshape(peers, held, LANES).astype(jnp.bfloat16)
    for q in range(seqs):
        for s in range(blocks):
            out_ref[q * blocks + s, held:, :] = rs[pl.ds(s * held + q * part, part), :].astype(
                jnp.bfloat16
            )


def unpack_body(
    groups, home, gate, values, gate_out, values_out, filter_out, gate_made, values_made, sums, sems
):
    part = gate.shape[2]
    sums[...] = home[:, groups * part :, :].astype(jnp.float32)
    sends = [pltpu.make_async_copy(sums, filter_out, sems.at[2 * groups])]
    sends[-1].start()
    for q in range(groups):
        carried = home[:, q * part : (q + 1) * part, :].astype(jnp.float32)
        gate_made[q] = (carried * values[q].astype(jnp.float32)).astype(jnp.bfloat16)
        values_made[q] = (carried * gate[q].astype(jnp.float32)).astype(jnp.bfloat16)
        for i, (made, out) in enumerate(((gate_made, gate_out), (values_made, values_out))):
            sends.append(pltpu.make_async_copy(made.at[q], out.at[q], sems.at[2 * q + i]))
            sends[-1].start()
    for copy in sends:
        copy.wait()


def correlate(arrived, seqs):
    peers, rows, _ = arrived.shape
    blocks = peers // seqs
    part = rows // (2 * seqs + 2)
    held = seqs * part
    whole = pl.BlockSpec(memory_space=pltpu.VMEM)
    return pl.pallas_call(
        functools.partial(correlate_body, seqs, blocks, UNROLL),
        out_shape=jax.ShapeDtypeStruct((peers, held + part, LANES), jnp.bfloat16),
        in_specs=[whole],
        out_specs=whole,
        scratch_shapes=[
            pltpu.VMEM((peers * held, LANES), jnp.float32),
            pltpu.VMEM((peers * held, LANES), jnp.float32),
            pltpu.VMEM((blocks * held, LANES), jnp.float32),
            pltpu.VMEM((peers * held, LANES), jnp.float32),
            pltpu.VMEM((blocks * held, LANES), jnp.float32),
            pltpu.VMEM((UNROLL * (LANES // REACH) * 2 * peers, LANES), jnp.float32),
            *[
                pltpu.VMEM((UNROLL, blocks, LANES // REACH * peers, LANES), jnp.bfloat16),
                pltpu.VMEM((UNROLL, blocks, 2 * REACH, LANES), jnp.bfloat16),
                pltpu.VMEM((UNROLL, REACH, LANES // REACH * peers), jnp.bfloat16),
            ]
            * 2,
        ],
        cost_estimate=pl.CostEstimate(
            flops=6 * held * LANES * blocks * LANES * peers, bytes_accessed=4 * arrived.size, transcendentals=0
        ),
    )(arrived)


def exchange(array):
    return lax.all_to_all(array, ("dp", "seq"), split_axis=0, concat_axis=0, tiled=True)


def direct_shards(gate_in, values_in, out_grad, filter_taps):
    groups = lax.axis_size("dp")
    peers = groups * lax.axis_size("seq")
    channels = gate_in.shape[1]
    part = channels // (groups * peers)
    shape = (groups, peers, part, LANES)
    gate, values, grad = (array.reshape(shape) for array in (gate_in, values_in, out_grad))
    taps = filter_taps.reshape(shape)
    pieces = math.gcd(peers, PIECES)
    own = lax.axis_index("dp").astype(jnp.int32).reshape(1)
    far = pl.BlockSpec(memory_space=pl.ANY)
    half = pltpu.VMEM(shape, jnp.bfloat16)
    packed = pl.pallas_call(
        functools.partial(pack_body, groups, pieces),
        out_shape=jax.ShapeDtypeStruct((peers, (2 * groups + 2) * part, LANES), jnp.bfloat16),
        in_specs=[pl.BlockSpec(memory_space=pltpu.SMEM), far, far, far, far],
        out_specs=far,
        scratch_shapes=[
            half,
            half,
            pltpu.VMEM(shape[1:], jnp.float32),
            pltpu.VMEM((peers, (2 * groups + 2) * part, LANES), jnp.bfloat16),
            pltpu.SemaphoreType.DMA((pieces, groups + 3)),
            pltpu.SemaphoreType.DMA((pieces,)),
        ],
    )(own, gate, values, grad, taps)
    near = functools.partial(pltpu.with_memory_space_constraint, memory_space=pltpu.VMEM)
    arrived = near(exchange(packed))
    made = correlate(arrived, groups)
    home = near(exchange(made))
    wide = jax.ShapeDtypeStruct(shape, jnp.bfloat16)
    local = pl.BlockSpec(memory_space=pltpu.VMEM)
    grad_gate, grad_values, grad_filter = pl.pallas_call(
        functools.partial(unpack_body, groups),
        out_shape=(wide, wide, jax.ShapeDtypeStruct(shape[1:], jnp.float32)),
        in_specs=[local, local, local],
        out_specs=(far, far, far),
        scratch_shapes=[
            half,
            half,
            pltpu.VMEM(shape[1:], jnp.float32),
            pltpu.SemaphoreType.DMA((2 * groups + 1,)),
        ],
    )(home, near(gate), near(values))
    return (
        grad_gate.reshape(gate_in.shape),
        grad_values.reshape(gate_in.shape),
        grad_filter.reshape(channels // groups, LANES),
    )


def shards(gate_in, values_in, out_grad, filter_taps):
    groups = lax.axis_size("dp")
    peers = groups * lax.axis_size("seq")
    channels, shard_len = gate_in.shape[1:]
    part = channels // (groups * peers)
    fits = 24 * channels * LANES * groups <= ROOM
    if shard_len == LANES and channels == part * groups * peers and part % SUBLANES == 0 and fits:
        return direct_shards(gate_in, values_in, out_grad, filter_taps)
    return spectral_shards(gate_in, values_in, out_grad, filter_taps)


def solution(mesh):
    return jax.shard_map(
        shards,
        mesh=mesh,
        in_specs=(P("dp", None, "seq"), P("dp", None, "seq"), P("dp", None, "seq"), P(None, "seq")),
        out_specs=(P("dp", None, "seq"), P("dp", None, "seq"), P("dp", "seq")),
        check_vma=False,
    )
```

```python
import functools
import math

import jax
import jax.numpy as jnp
from jax import lax
from jax.experimental import pallas as pl
from jax.experimental.pallas import tpu as pltpu
from jax.sharding import PartitionSpec as P

LANES = 128
SUBLANES = 16
REACH = 32
PIECES = 4
ROOM = 40 * 2**20

precise = lax.Precision.HIGHEST
coarse = lax.Precision.HIGH


def spin_tables(count_in, count_out, period):
    rows = lax.broadcasted_iota(jnp.int32, (count_in, count_out), 0)
    cols = lax.broadcasted_iota(jnp.int32, (count_in, count_out), 1)
    phase = (rows * cols % period).astype(jnp.float32) * (2.0 * math.pi / period)
    return (jnp.cos(phase), jnp.sin(phase))


def make_tables(length, columns):
    rows_in = length // columns
    rows_out = 2 * rows_in
    first_cos, first_sin = spin_tables(rows_in, rows_out, rows_out)
    turn = spin_tables(rows_out, columns, 2 * length)
    last_cos, last_sin = spin_tables(columns, columns, columns)
    first_fwd = jnp.concatenate([first_cos, -first_sin], axis=1)
    last_fwd = jnp.concatenate(
        [
            jnp.concatenate([last_cos, -last_sin], axis=1),
            jnp.concatenate([last_sin, last_cos], axis=1),
        ],
        axis=0,
    )
    last_inv = jnp.concatenate(
        [
            jnp.concatenate([last_cos.T, last_sin.T], axis=1),
            jnp.concatenate([-last_sin.T, last_cos.T], axis=1),
        ],
        axis=0,
    )
    first_inv = jnp.concatenate(
        [
            jnp.concatenate([first_cos.T, first_sin.T], axis=1),
            jnp.concatenate([-first_sin.T, first_cos.T], axis=1),
        ],
        axis=0,
    )
    return (first_fwd, turn, last_fwd, last_inv, first_inv)


def spectrum(signal, tables, columns, first_precision):
    first_fwd, (turn_cos, turn_sin), last_fwd, last_inv, first_inv = tables
    held, length = signal.shape
    half = turn_cos.shape[0]
    grid = signal.reshape(held, length // columns, columns)
    part = jnp.einsum("cmn,mk->ckn", grid, first_fwd, precision=first_precision)
    part_real = part[:, :half]
    part_imag = part[:, half:]
    turned = jnp.concatenate(
        [part_real * turn_cos + part_imag * turn_sin, part_imag * turn_cos - part_real * turn_sin],
        axis=2,
    )
    out = jnp.einsum("ckn,nj->ckj", turned, last_fwd, precision=first_precision)
    return (out[:, :, :columns], out[:, :, columns:])


def to_signal(spec_real, spec_imag, tables, length):
    first_fwd, (turn_cos, turn_sin), last_fwd, last_inv, first_inv = tables
    held = spec_real.shape[0]
    columns = spec_real.shape[2]
    rows_in = length // columns
    stacked = jnp.concatenate([spec_real, spec_imag], axis=2)
    back = jnp.einsum("ckj,jn->ckn", stacked, last_inv, precision=coarse)
    back_real = back[:, :, :columns]
    back_imag = back[:, :, columns:]
    turned = jnp.concatenate(
        [back_real * turn_cos - back_imag * turn_sin, back_imag * turn_cos + back_real * turn_sin],
        axis=1,
    )
    factor = 1.0 / (2 * length)
    both = jnp.einsum("ckn,km->cmn", turned, first_inv, precision=coarse) * factor
    real_part = both[:, :rows_in]
    imag_part = both[:, rows_in:]
    return (real_part.reshape(held, length), imag_part.reshape(held, length))


def spectral_shards(gate_in, values_in, out_grad, filter_taps):
    seq_count = lax.axis_size("seq")
    group_count = lax.axis_size("dp")
    channels = gate_in.shape[1]
    shard_len = gate_in.shape[2]
    length = shard_len * seq_count
    quarter = channels // group_count
    per_block = quarter // seq_count
    held_channels = group_count * per_block
    columns = 128 if length % 128 == 0 and length >= 8192 else 32
    tables = make_tables(length, columns)
    gate_wide = gate_in[0].astype(jnp.float32)
    values_wide = values_in[0].astype(jnp.float32)
    mixed = (gate_wide * values_wide).astype(jnp.bfloat16)
    grad_rows, mixed_rows = (
        lax.all_to_all(
            out_grad[0].reshape(group_count, quarter, shard_len),
            "seq",
            split_axis=1,
            concat_axis=2,
            tiled=True,
        ),
        lax.all_to_all(
            mixed.reshape(group_count, quarter, shard_len),
            "seq",
            split_axis=1,
            concat_axis=2,
            tiled=True,
        ),
    )
    filter_grouped = filter_taps.reshape(group_count, quarter, shard_len)
    filter_rows = lax.all_to_all(filter_grouped, "seq", split_axis=1, concat_axis=2, tiled=True)
    grad_real, grad_imag = spectrum(
        grad_rows.reshape(held_channels, length).astype(jnp.float32), tables, columns, coarse
    )
    mix_real, mix_imag = spectrum(
        mixed_rows.reshape(held_channels, length).astype(jnp.float32), tables, columns, coarse
    )
    tap_real, tap_imag = spectrum(
        filter_rows.reshape(held_channels, length), tables, columns, precise
    )
    carry_real = tap_real * grad_real + tap_imag * grad_imag
    carry_imag = tap_real * grad_imag - tap_imag * grad_real
    lag_real = grad_real * mix_real + grad_imag * mix_imag
    lag_imag = grad_imag * mix_real - grad_real * mix_imag
    carried, lagged = to_signal(carry_real - lag_imag, carry_imag + lag_real, tables, length)
    carried = carried.astype(jnp.bfloat16).reshape(group_count, per_block, length)
    returned = lax.all_to_all(carried, "seq", split_axis=2, concat_axis=1, tiled=True)
    carried_home = returned.reshape(channels, shard_len).astype(jnp.float32)
    lagged = lagged.reshape(group_count, per_block, length)
    summed = lax.psum_scatter(lagged, "dp", scatter_dimension=0, tiled=True)
    grad_filter = lax.all_to_all(summed, "seq", split_axis=2, concat_axis=1, tiled=True).reshape(
        quarter, shard_len
    )
    grad_gate = (carried_home * values_wide).astype(jnp.bfloat16)[None]
    grad_values = (carried_home * gate_wide).astype(jnp.bfloat16)[None]
    return (grad_gate, grad_values, grad_filter)


def pack_body(
    groups, pieces, own_ref, gate_ref, values_ref, grad_ref, taps_ref, out_ref,
    gate, values, taps, made, in_sems, out_sems,
):
    peers, part = gate.shape[1:3]
    size = peers // pieces
    loads = []
    for j in range(pieces):
        own = pl.ds(j * size, size)
        pairs = [
            (gate_ref.at[:, own], gate.at[:, own]),
            (values_ref.at[:, own], values.at[:, own]),
            (taps_ref.at[own_ref[0], own], taps.at[own]),
        ]
        pairs += [
            (grad_ref.at[q, own], made.at[own, pl.ds(q * part, part), :]) for q in range(groups)
        ]
        loads.append(
            [
                pltpu.make_async_copy(source, target, in_sems.at[j, i])
                for i, (source, target) in enumerate(pairs)
            ]
        )
    for copies in loads:
        for copy in copies:
            copy.start()
    sends = []
    for j in range(pieces):
        own = slice(j * size, (j + 1) * size)
        for copy in loads[j][:3]:
            copy.wait()
        for q in range(groups):
            product = gate[q, own].astype(jnp.float32) * values[q, own].astype(jnp.float32)
            made[own, (groups + q) * part : (groups + q + 1) * part, :] = product.astype(jnp.bfloat16)
        high = taps[own].astype(jnp.bfloat16)
        made[own, 2 * groups * part : (2 * groups + 1) * part, :] = high
        made[own, (2 * groups + 1) * part :, :] = (taps[own] - high.astype(jnp.float32)).astype(
            jnp.bfloat16
        )
        for copy in loads[j][3:]:
            copy.wait()
        rows = pl.ds(j * size, size)
        sends.append(pltpu.make_async_copy(made.at[rows], out_ref.at[rows], out_sems.at[j]))
        sends[-1].start()
    for copy in sends:
        copy.wait()


def correlate_body(seqs, blocks, unroll, in_ref, out_ref, gs, ms, fs, cs, rs, pads, hs0, ts0, tn0, hs1, ts1, tn1, stage, sems):
    peers = seqs * blocks
    part = in_ref.shape[1] // (2 * seqs + 2)
    held = seqs * part
    steps = LANES // REACH
    near = lax.broadcasted_iota(jnp.int32, (REACH, LANES), 0)
    lane = lax.broadcasted_iota(jnp.int32, (REACH, LANES), 1)
    flip = jnp.where(lane % REACH + near == REACH - 1, 1.0, 0.0).astype(jnp.bfloat16)
    ours = lax.broadcasted_iota(jnp.int32, (peers, LANES), 1) // REACH
    inside = lane + REACH - 1 - near < LANES
    ahead = lane >= near
    deep = lax.broadcasted_iota(jnp.int32, (blocks, LANES), 0)
    thin = lax.broadcasted_iota(jnp.int32, (blocks, LANES), 1)
    across = (((1,), (1,)), ((), ()))
    span = blocks * held
    for b in range(seqs):
        mine = slice(b * blocks, (b + 1) * blocks)
        gs[pl.ds(b * span, span), :] = (
            in_ref[mine, :held, :].astype(jnp.float32).reshape(span, LANES)
        )
        ms[pl.ds(b * span, span), :] = (
            in_ref[mine, held : 2 * held, :].astype(jnp.float32).reshape(span, LANES)
        )
        for s in range(blocks):
            high = in_ref[b * blocks + s, 2 * held : 2 * held + part, :].astype(jnp.float32)
            low = in_ref[b * blocks + s, 2 * held + part :, :].astype(jnp.float32)
            fs[pl.ds(s * held + b * part, part), :] = high + low
    pads[...] = jnp.zeros_like(pads)

    def at(u, q, b):
        return ((u * steps + q) * seqs + b) * 2 * blocks

    def turn_over(group, tn):
        for u in range(unroll):
            c = group * unroll + u
            mixed = ms[pl.ds(c, peers, stride=held), :]
            mixed = jnp.concatenate(
                [jnp.where(ours == q, mixed, 0.0).astype(jnp.bfloat16) for q in range(steps)], axis=0
            )
            tn[u] = lax.dot_general(
                flip, mixed, across, preferred_element_type=jnp.float32
            ).astype(jnp.bfloat16)

    def build(group, hs, ts):
        for u in range(unroll):
            c = group * unroll + u
            for b in range(seqs):
                pads[pl.ds(at(u, 0, b), blocks), :] = gs[pl.ds(b * span + c, blocks, stride=held), :]
        for u in range(unroll):
            for q in range(1, steps):
                for b in range(seqs):
                    here = pads[pl.ds(at(u, 0, b), blocks), :]
                    then = pads[pl.ds(at(u, 0, b) + 1, blocks), :]
                    pads[pl.ds(at(u, q, b), blocks), :] = pltpu.roll(
                        jnp.where(thin >= q * REACH, here, then), LANES - q * REACH, 1
                    )
        for u in range(unroll):
            c = group * unroll + u
            taps = fs[pl.ds(c, blocks, stride=held), :]
            before = jnp.zeros((REACH, LANES), jnp.float32)
            for k in range(blocks):
                turn = pltpu.roll(
                    jnp.broadcast_to(taps[k : k + 1, :], (REACH, LANES)),
                    0,
                    1,
                    stride=1,
                    stride_axis=0,
                )
                block = jnp.where(ahead, turn, before)
                before = turn
                top = block.astype(jnp.bfloat16)
                ts[u, k, :REACH, :] = top
                ts[u, k, REACH:, :] = (block - top.astype(jnp.float32)).astype(jnp.bfloat16)
        for u in range(unroll):
            for q in range(steps):
                for k in range(blocks):
                    hs[u, k, q * peers : (q + 1) * peers, :] = jnp.concatenate(
                        [pads[pl.ds(at(u, q, b) + k, blocks), :] for b in range(seqs)], axis=0
                    ).astype(jnp.bfloat16)

    def joined(ref, u):
        return jnp.concatenate([ref[u, k] for k in range(blocks)], axis=1)

    def merged(parts):
        gap = 1
        while len(parts) > 1:
            keep = deep & gap == 0
            parts = [
                jnp.where(keep, x, y) + pltpu.roll(jnp.where(keep, y, x), gap, 0)
                for x, y in zip(parts[0::2], parts[1::2])
            ]
            gap *= 2
        return parts[0]

    def multiply(group, hs, ts, tn):
        for u in range(unroll):
            c = group * unroll + u
            gram = jnp.dot(tn[u], joined(hs, u), preferred_element_type=jnp.float32)
            later = jnp.zeros((REACH, LANES), jnp.float32)
            sums = []
            for k in reversed(range(blocks)):
                turn = pltpu.roll(
                    gram[:, k * LANES : (k + 1) * LANES],
                    LANES + 1 - REACH,
                    1,
                    stride=1,
                    stride_axis=0,
                )
                picked = jnp.where(inside, turn, later)
                sums.append(sum(picked[i : i + blocks] for i in range(0, REACH, blocks)))
                later = turn
            rs[pl.ds(c, blocks, stride=held), :] = merged(sums[::-1])
        for u in range(unroll):
            c = group * unroll + u
            short = lax.dot_general(
                joined(hs, u), joined(ts, u), across, preferred_element_type=jnp.float32
            )
            short = jnp.concatenate(
                [short, jnp.zeros((steps * peers, LANES - 2 * REACH), jnp.float32)], axis=1
            )
            carried = None
            for q in range(steps):
                mine = short[q * peers : (q + 1) * peers]
                both = pltpu.roll(mine, q * REACH, 1) if q else mine
                back = (q - 1) % steps
                both = both + (pltpu.roll(mine, back * REACH, 1) if back else mine)
                carried = both if carried is None else jnp.where(ours == q, both, carried)
            cs[pl.ds(c, peers, stride=held), :] = carried

    total = held // unroll
    turn_over(0, tn0)
    build(0, hs0, ts0)

    def twice(i, carry):
        turn_over(2 * i + 1, tn1)
        multiply(2 * i, hs0, ts0, tn0)
        build(2 * i + 1, hs1, ts1)
        after = jnp.minimum(2 * i + 2, total - 1)
        turn_over(after, tn0)
        multiply(2 * i + 1, hs1, ts1, tn1)
        build(after, hs0, ts0)
        for p in range(peers):
            mine = cs[pl.ds(pl.multiple_of(p * held + i * part, part), part), :]
            stage[i, p] = mine.astype(jnp.bfloat16)
        pltpu.make_async_copy(
            stage.at[i], out_ref.at[:, pl.ds(pl.multiple_of(i * part, part), part), :], sems.at[i]
        ).start()
        return carry

    lax.fori_loop(0, total // 2, twice, 0)
    for q in range(seqs):
        for b in range(blocks):
            stage[seqs, q * blocks + b] = rs[pl.ds(b * held + q * part, part), :].astype(
                jnp.bfloat16
            )
    sends = [
        pltpu.make_async_copy(
            stage.at[q], out_ref.at[:, pl.ds(q * part, part), :], sems.at[q]
        )
        for q in range(seqs + 1)
    ]
    sends[seqs].start()
    for copy in sends:
        copy.wait()


def unpack_body(
    groups, home, gate, values, gate_out, values_out, filter_out, gate_made, values_made, sums, sems
):
    part = gate.shape[2]
    sums[...] = home[:, groups * part :, :].astype(jnp.float32)
    sends = [pltpu.make_async_copy(sums, filter_out, sems.at[2 * groups])]
    sends[-1].start()
    for q in range(groups):
        carried = home[:, q * part : (q + 1) * part, :].astype(jnp.float32)
        gate_made[q] = (carried * values[q].astype(jnp.float32)).astype(jnp.bfloat16)
        values_made[q] = (carried * gate[q].astype(jnp.float32)).astype(jnp.bfloat16)
        for i, (made, out) in enumerate(((gate_made, gate_out), (values_made, values_out))):
            sends.append(pltpu.make_async_copy(made.at[q], out.at[q], sems.at[2 * q + i]))
            sends[-1].start()
    for copy in sends:
        copy.wait()


def correlate(arrived, seqs):
    peers, rows, _ = arrived.shape
    blocks = peers // seqs
    part = rows // (2 * seqs + 2)
    held = seqs * part
    whole = pl.BlockSpec(memory_space=pltpu.VMEM)
    return pl.pallas_call(
        functools.partial(correlate_body, seqs, blocks, (part // 2)),
        out_shape=jax.ShapeDtypeStruct((peers, held + part, LANES), jnp.bfloat16),
        in_specs=[whole],
        out_specs=pl.BlockSpec(memory_space=pl.ANY),
        scratch_shapes=[
            pltpu.VMEM((peers * held, LANES), jnp.float32),
            pltpu.VMEM((peers * held, LANES), jnp.float32),
            pltpu.VMEM((blocks * held, LANES), jnp.float32),
            pltpu.VMEM((peers * held, LANES), jnp.float32),
            pltpu.VMEM((blocks * held, LANES), jnp.float32),
            pltpu.VMEM(((part // 2) * (LANES // REACH) * 2 * peers, LANES), jnp.float32),
            *[
                pltpu.VMEM(((part // 2), blocks, LANES // REACH * peers, LANES), jnp.bfloat16),
                pltpu.VMEM(((part // 2), blocks, 2 * REACH, LANES), jnp.bfloat16),
                pltpu.VMEM(((part // 2), REACH, LANES // REACH * peers), jnp.bfloat16),
            ]
            * 2,
            pltpu.VMEM((seqs + 1, peers, part, LANES), jnp.bfloat16),
            pltpu.SemaphoreType.DMA((seqs + 1,)),
        ],
        cost_estimate=pl.CostEstimate(
            flops=6 * held * LANES * blocks * LANES * peers, bytes_accessed=4 * arrived.size, transcendentals=0
        ),
    )(arrived)


def exchange(array):
    return lax.all_to_all(array, ("dp", "seq"), split_axis=0, concat_axis=0, tiled=True)


def direct_shards(gate_in, values_in, out_grad, filter_taps):
    groups = lax.axis_size("dp")
    peers = groups * lax.axis_size("seq")
    channels = gate_in.shape[1]
    part = channels // (groups * peers)
    shape = (groups, peers, part, LANES)
    gate, values, grad = (array.reshape(shape) for array in (gate_in, values_in, out_grad))
    taps = filter_taps.reshape(shape)
    pieces = math.gcd(peers, PIECES)
    own = lax.axis_index("dp").astype(jnp.int32).reshape(1)
    far = pl.BlockSpec(memory_space=pl.ANY)
    half = pltpu.VMEM(shape, jnp.bfloat16)
    packed = pl.pallas_call(
        functools.partial(pack_body, groups, pieces),
        out_shape=jax.ShapeDtypeStruct((peers, (2 * groups + 2) * part, LANES), jnp.bfloat16),
        in_specs=[pl.BlockSpec(memory_space=pltpu.SMEM), far, far, far, far],
        out_specs=far,
        scratch_shapes=[
            half,
            half,
            pltpu.VMEM(shape[1:], jnp.float32),
            pltpu.VMEM((peers, (2 * groups + 2) * part, LANES), jnp.bfloat16),
            pltpu.SemaphoreType.DMA((pieces, groups + 3)),
            pltpu.SemaphoreType.DMA((pieces,)),
        ],
    )(own, gate, values, grad, taps)
    near = functools.partial(pltpu.with_memory_space_constraint, memory_space=pltpu.VMEM)
    arrived = near(exchange(packed))
    made = correlate(arrived, groups)
    home = near(exchange(made))
    wide = jax.ShapeDtypeStruct(shape, jnp.bfloat16)
    local = pl.BlockSpec(memory_space=pltpu.VMEM)
    grad_gate, grad_values, grad_filter = pl.pallas_call(
        functools.partial(unpack_body, groups),
        out_shape=(wide, wide, jax.ShapeDtypeStruct(shape[1:], jnp.float32)),
        in_specs=[local, local, local],
        out_specs=(far, far, far),
        scratch_shapes=[
            half,
            half,
            pltpu.VMEM(shape[1:], jnp.float32),
            pltpu.SemaphoreType.DMA((2 * groups + 1,)),
        ],
    )(home, near(gate), near(values))
    return (
        grad_gate.reshape(gate_in.shape),
        grad_values.reshape(gate_in.shape),
        grad_filter.reshape(channels // groups, LANES),
    )


def shards(gate_in, values_in, out_grad, filter_taps):
    groups = lax.axis_size("dp")
    peers = groups * lax.axis_size("seq")
    channels, shard_len = gate_in.shape[1:]
    part = channels // (groups * peers)
    fits = 24 * channels * LANES * groups <= ROOM
    if shard_len == LANES and channels == part * groups * peers and part % SUBLANES == 0 and fits:
        return direct_shards(gate_in, values_in, out_grad, filter_taps)
    return spectral_shards(gate_in, values_in, out_grad, filter_taps)


def solution(mesh):
    return jax.shard_map(
        shards,
        mesh=mesh,
        in_specs=(P("dp", None, "seq"), P("dp", None, "seq"), P("dp", None, "seq"), P(None, "seq")),
        out_specs=(P("dp", None, "seq"), P("dp", None, "seq"), P("dp", "seq")),
        check_vma=False,
    )
```
